32 devices in a mesh: chan: 8 (over z, y), pair: 4 (over x, core).
Axes of the slice: x: 2, y: 2, z: 4, core: 2. Of those that a mesh axis runs over, the one named last changes fastest.
Arguments:
- voltages: bfloat16 [4, 16, 2, 34560], P('pair', 'chan'), may hold values from -6 to 6
- fir_taps: float32 [8, 256], replicated, may hold values from -2 to 2
Outputs:
- visibilities: float32 [128, 2, 64, 64], P('chan', None, 'pair')
The draws below stay inside these ranges and needn't reach their ends.
All inputs are finite; a program needn't handle non-finite values.
Results may differ from the reference program's by a relative error of at most 0.0036.
Values may be sent and summed in bfloat16 or wider, within the bound.
No kernel may reach another device: no remote copies, remote signals or barrier semaphores. Data moves between devices by JAX's collectives and lax.ppermute only.
A program may use at most 64 MiB of HBM per device.

```python
import math
import jax
import jax.numpy as jnp
from jax import lax

C = 128
P_SIZE = 8
S = 128
NB = 2
A = 64
N_PAIR = 4


def block_levels(rng, shape, split, low, largest):
    factor_of, own = 1.0, jax.random.fold_in(rng, 6)
    for position, blocks in split:
        heights = jnp.exp(jax.random.uniform(jax.random.fold_in(own, position), (blocks,), jnp.float32, low / len(split), largest / len(split)))
        factor_of = factor_of * jnp.repeat(heights, shape[position] // blocks).reshape([-1 if axis == position else 1 for axis in range(len(shape))])
    return factor_of


def bell_draw(rng, shape, deviation, reach, cuts=(), kind=jnp.bfloat16):
    level = block_levels(rng, shape, cuts, -0.22, 0.18) if cuts else 1.0
    drawn = jax.random.normal(rng, shape, jnp.float32) * deviation * level
    return jnp.minimum(jnp.maximum(drawn, -reach), reach).astype(kind)


def setup_inputs(seed: int = 0) -> dict:
    keys = jax.random.split(jax.random.key(seed), 3)
    return {
        "voltages": bell_draw(keys[0], (N_PAIR, A // N_PAIR, NB, (S + P_SIZE - 1) * 2 * C), 1.0, 6.0, ((0, 4), (1, 8))),
        "fir_taps": bell_draw(keys[1], (P_SIZE, 2 * C), P_SIZE ** -0.5, 2.0, (), jnp.float32),
    }


def dft_rows(channels):
    frame = 2 * channels
    row_index = jnp.arange(2 * channels, dtype=jnp.int32)
    col_index = jnp.arange(frame, dtype=jnp.int32)
    freq_index = row_index // 2
    phases = freq_index[:, None] * col_index[None, :] % frame
    angles = phases.astype(jnp.float32) * (2.0 * math.pi / frame)
    chosen = jnp.where((row_index % 2 == 0)[:, None], jnp.cos(angles), -jnp.sin(angles))
    return chosen * (1.0 / math.sqrt(frame))

def rotate_parts(block_data, spectra_len):
    shaped = block_data.reshape(block_data.shape[:-1] + (block_data.shape[-1] // (2 * spectra_len), 2, spectra_len))
    rotated = jnp.stack([-shaped[..., 1, :], shaped[..., 0, :]], axis=-2)
    return rotated.reshape(block_data.shape)

def reference(voltages, fir_taps):
    frame = 2 * C
    samples = voltages.reshape(A, NB, (S + P_SIZE - 1) * frame)
    transform = dft_rows(C)
    pieces = []
    for batch in range(NB):
        framed = samples[:, batch].astype(jnp.float32).reshape(A, S + P_SIZE - 1, frame)
        filtered = jnp.zeros((A, S, frame), jnp.float32)
        for tap in range(P_SIZE):
            filtered = filtered + fir_taps[tap][None, None, :] * framed[:, tap:tap + S, :]
        spectra = jnp.einsum('wn,asn->aws', transform, filtered, precision=lax.Precision.HIGHEST)
        pieces.append(spectra.reshape(A, C, 2 * S).astype(jnp.bfloat16))
    allspec = jnp.concatenate(pieces, axis=2)
    by_channel = jnp.transpose(allspec, (1, 0, 2))

    def per_channel(block_data):
        as_float = block_data.astype(jnp.float32)
        rotated = rotate_parts(as_float, S)
        real_part = jnp.dot(as_float, as_float.T, precision=lax.Precision.HIGHEST, preferred_element_type=jnp.float32)
        imag_part = jnp.dot(as_float, rotated.T, precision=lax.Precision.HIGHEST, preferred_element_type=jnp.float32)
        return jnp.stack([real_part, imag_part])
    summed = lax.map(per_channel, by_channel)
    return summed * (1.0 / math.sqrt(NB * S))
```

```python
import functools
import math

import jax
import jax.numpy as jnp
import numpy as np
from jax import lax
from jax.experimental import pallas as pl
from jax.experimental.pallas import tpu as pltpu
from jax.sharding import PartitionSpec as P

LANES = 128
VMEM = pltpu.MemorySpace.VMEM


def dft_rows(channels):
    frame = 2 * channels
    row_index = jnp.arange(2 * channels, dtype=jnp.int32)
    col_index = jnp.arange(frame, dtype=jnp.int32)
    freq_index = row_index // 2
    phases = freq_index[:, None] * col_index[None, :] % frame
    angles = phases.astype(jnp.float32) * (2.0 * math.pi / frame)
    chosen = jnp.where((row_index % 2 == 0)[:, None], jnp.cos(angles), -jnp.sin(angles))
    return chosen * (1.0 / math.sqrt(frame))


def dft_table(channels):
    frame = 2 * channels
    row = np.arange(frame)
    phases = (row // 2)[:, None] * np.arange(frame)[None, :] % frame
    angles = phases * (2.0 * np.pi / frame)
    chosen = np.where((row % 2 == 0)[:, None], np.cos(angles), -np.sin(angles))
    return chosen / np.sqrt(frame)


def channelize(sample_rows, fir_taps, transform, spectra_len):
    tap_count, frame = fir_taps.shape
    channels = frame // 2
    framed = sample_rows.astype(jnp.float32).reshape(
        sample_rows.shape[0], spectra_len + tap_count - 1, frame
    )
    filtered = jnp.zeros((sample_rows.shape[0], spectra_len, frame), jnp.float32)
    for tap in range(tap_count):
        filtered = filtered + fir_taps[tap][None, None, :] * framed[:, tap : tap + spectra_len, :]
    spectra = jnp.einsum("wn,asn->aws", transform, filtered, precision=lax.Precision.HIGHEST)
    return spectra.reshape(sample_rows.shape[0], channels, 2 * spectra_len).astype(jnp.bfloat16)


def correlate(own_rows, columns, spectra_len):
    blocks = columns.shape[2] // (2 * spectra_len)
    shaped = columns.reshape(columns.shape[0], columns.shape[1], blocks, 2, spectra_len)
    rotated = jnp.stack([-shaped[:, :, :, 1, :], shaped[:, :, :, 0, :]], axis=3).reshape(
        columns.shape
    )
    stacked = jnp.concatenate([columns, rotated], axis=0)
    stacked = jnp.transpose(stacked, (1, 0, 2))
    own_first = jnp.transpose(own_rows, (1, 0, 2))
    product = jnp.einsum("cik,cjk->cij", own_first, stacked, preferred_element_type=jnp.float32)
    count = columns.shape[0]
    product = product.reshape(product.shape[0], product.shape[1], 2, count)
    return jnp.transpose(product, (0, 2, 1, 3))


def gathered_shards(voltages, fir_taps):
    samples = voltages[0]
    batch_count = samples.shape[1]
    tap_count, frame = fir_taps.shape
    spectra_len = samples.shape[2] // frame - tap_count + 1
    transform = dft_rows(frame // 2)
    pieces = [
        channelize(samples[:, batch], fir_taps, transform, spectra_len)
        for batch in range(batch_count)
    ]
    spectra = jnp.concatenate(pieces, axis=2)[None]
    turned = lax.all_to_all(spectra, "chan", split_axis=2, concat_axis=1, tiled=True)
    own_rows = turned[0]
    arrived = lax.all_gather(turned, "pair", axis=0, tiled=True)
    flat = arrived.reshape(arrived.shape[0] * arrived.shape[1], arrived.shape[2], arrived.shape[3])
    summed = correlate(own_rows, flat, spectra_len)
    return summed * (1.0 / math.sqrt(batch_count * spectra_len))


def channelize_kernel(antennas, batches, frames, v_ref, taps_ref, dft_ref, o_ref, x_ref, f_ref):
    taps, frame = taps_ref.shape
    parts = frame // LANES
    step = parts * batches
    spectra = frames - taps + 1
    x_ref[...] = v_ref[...].astype(jnp.float32)
    for a in range(antennas):
        for b in range(batches):
            for h in range(parts):
                lanes = slice(h * LANES, (h + 1) * LANES)
                total = None
                for p in range(taps):
                    first = (a * frames + p) * step + h * batches + b
                    term = taps_ref[p : p + 1, lanes] * x_ref[pl.ds(first, spectra, stride=step), :]
                    total = term if total is None else total + term
                f_ref[a, b * spectra : (b + 1) * spectra, lanes] = total.astype(jnp.bfloat16)
        spec = lax.dot_general(
            dft_ref[...], f_ref[a], (((1,), (1,)), ((), ())), preferred_element_type=jnp.float32
        )
        o_ref[:, a, :, :] = spec.astype(jnp.bfloat16).reshape(
            o_ref.shape[0], o_ref.shape[2], o_ref.shape[3]
        )


def correlate_kernel(groups, blocks, antennas, channels, scale, y_ref, *refs):
    outs, scr, vis = refs[: blocks], refs[blocks], refs[blocks + 1]
    rows = antennas * channels * 2
    width = y_ref.shape[1]
    parts = width // LANES
    total = groups * blocks * antennas
    for g in range(groups):
        for q in range(blocks):
            src = y_ref[(g * blocks + q) * rows : (g * blocks + q + 1) * rows, :].astype(jnp.float32)
            for t in range(parts):
                scr[t, (q * groups + g) * rows : (q * groups + g + 1) * rows, :] = src[
                    :, t * LANES : (t + 1) * LANES
                ]
    for c in range(channels):
        re = [scr[t, pl.ds(2 * c, total, stride=2 * channels), :] for t in range(parts)]
        im = [scr[t, pl.ds(2 * c + 1, total, stride=2 * channels), :] for t in range(parts)]
        own = jnp.concatenate(re + im, axis=1).astype(jnp.bfloat16)
        turned = jnp.concatenate([-x for x in im] + re, axis=1).astype(jnp.bfloat16)
        both = jnp.concatenate([own, turned], axis=0)
        prod = lax.dot_general(
            own, both, (((1,), (1,)), ((), ())), preferred_element_type=jnp.float32
        )
        vis[:, c, :, :] = (prod * scale).reshape(blocks, total // blocks, 2 * total)
    me = lax.axis_index("pair")
    for j in range(blocks):
        outs[j][...] = vis[me ^ j]


def place_kernel(blocks, *refs):
    ins, o_ref = refs[:blocks], refs[blocks]
    channels = ins[0].shape[0]
    columns = ins[0].shape[2] // 2
    me = lax.axis_index("pair")
    for j in range(blocks):
        at = pl.ds((me ^ j) * channels, channels)
        block = ins[j][...]
        o_ref[at, 0, :, :] = block[:, :, :columns]
        o_ref[at, 1, :, :] = block[:, :, columns:]


def exchanged_shards(groups, blocks, voltages, fir_taps):
    _, antennas, batches, length = voltages.shape
    taps, frame = fir_taps.shape
    frames = length // frame
    spectra = frames - taps + 1
    parts = frame // LANES
    devices = groups * blocks
    channels = frame // 2 // devices
    total = devices * antennas
    rows = antennas * frames * parts * batches
    lined = voltages.reshape(antennas, batches, frames * parts, LANES)
    lined = jnp.transpose(lined, (0, 2, 1, 3)).reshape(rows, LANES)
    table = jnp.asarray(dft_table(frame // 2), jnp.bfloat16)
    vmem = pl.BlockSpec(memory_space=VMEM)
    sent = pl.pallas_call(
        functools.partial(channelize_kernel, antennas, batches, frames),
        out_shape=jax.ShapeDtypeStruct(
            (devices, antennas, 2 * channels, batches * spectra), jnp.bfloat16
        ),
        in_specs=[vmem] * 3,
        out_specs=vmem,
        scratch_shapes=[
            pltpu.VMEM((rows, LANES), jnp.float32),
            pltpu.VMEM((antennas, batches * spectra, frame), jnp.bfloat16),
        ],
        name="channelize",
    )(lined, fir_taps, table)
    sent = sent.reshape(devices, antennas * 2 * channels, batches * spectra)
    turned = lax.all_to_all(sent, ("chan", "pair"), 0, 0, tiled=True)
    own_shape = jax.ShapeDtypeStruct((channels, total // blocks, 2 * total), jnp.float32)
    pieces = pl.pallas_call(
        functools.partial(
            correlate_kernel,
            groups,
            blocks,
            antennas,
            channels,
            1.0 / math.sqrt(batches * spectra),
        ),
        out_shape=[own_shape] * blocks,
        in_specs=[vmem],
        out_specs=[vmem] * blocks,
        scratch_shapes=[
            pltpu.VMEM(
                (batches * spectra // LANES, devices * antennas * 2 * channels, LANES), jnp.float32
            ),
            pltpu.VMEM((blocks, channels, total // blocks, 2 * total), jnp.float32),
        ],
        name="correlate",
    )(turned.reshape(devices * antennas * 2 * channels, batches * spectra))
    arrived = [pieces[0]] + [
        lax.ppermute(pieces[j], "pair", [(i, i ^ j) for i in range(blocks)])
        for j in range(1, blocks)
    ]
    return pl.pallas_call(
        functools.partial(place_kernel, blocks),
        out_shape=jax.ShapeDtypeStruct(
            (blocks * channels, 2, total // blocks, total), jnp.float32
        ),
        in_specs=[vmem] * blocks,
        out_specs=vmem,
        name="place",
    )(*arrived)


def solution(mesh):
    groups, blocks = mesh.shape["chan"], mesh.shape["pair"]
    in_specs = (P("pair", "chan", None, None), P())
    out_specs = P("chan", None, "pair", None)

    def shards(voltages, fir_taps):
        channels = fir_taps.shape[1] // 2
        spectra = voltages.shape[3] // fir_taps.shape[1] - fir_taps.shape[0] + 1
        if (
            channels % (groups * blocks) == 0
            and blocks & (blocks - 1) == 0
            and fir_taps.shape[1] % LANES == 0
            and spectra % LANES == 0
            and voltages.shape[1] * 2 * channels // (groups * blocks) % 16 == 0
        ):
            return exchanged_shards(groups, blocks, voltages, fir_taps)
        return gathered_shards(voltages, fir_taps)

    return jax.shard_map(shards, mesh=mesh, in_specs=in_specs, out_specs=out_specs, check_vma=False)
```

```python
import functools
import math

import jax
import jax.numpy as jnp
import numpy as np
from jax import lax
from jax.experimental import pallas as pl
from jax.experimental.pallas import tpu as pltpu
from jax.sharding import PartitionSpec as P

LANES = 128
LIMIT = 16 * 2**20
VMEM = pltpu.MemorySpace.VMEM


def dft_rows(channels):
    frame = 2 * channels
    row_index = jnp.arange(2 * channels, dtype=jnp.int32)
    col_index = jnp.arange(frame, dtype=jnp.int32)
    freq_index = row_index // 2
    phases = freq_index[:, None] * col_index[None, :] % frame
    angles = phases.astype(jnp.float32) * (2.0 * math.pi / frame)
    chosen = jnp.where((row_index % 2 == 0)[:, None], jnp.cos(angles), -jnp.sin(angles))
    return chosen * (1.0 / math.sqrt(frame))


def dft_table(channels):
    frame = 2 * channels
    row = np.arange(frame)
    phases = (row // 2)[:, None] * np.arange(frame)[None, :] % frame
    angles = phases * (2.0 * np.pi / frame)
    chosen = np.where((row % 2 == 0)[:, None], np.cos(angles), -np.sin(angles))
    return chosen / np.sqrt(frame)


def channelize(sample_rows, fir_taps, transform, spectra_len):
    tap_count, frame = fir_taps.shape
    channels = frame // 2
    framed = sample_rows.astype(jnp.float32).reshape(
        sample_rows.shape[0], spectra_len + tap_count - 1, frame
    )
    filtered = jnp.zeros((sample_rows.shape[0], spectra_len, frame), jnp.float32)
    for tap in range(tap_count):
        filtered = filtered + fir_taps[tap][None, None, :] * framed[:, tap : tap + spectra_len, :]
    spectra = jnp.einsum("wn,asn->aws", transform, filtered, precision=lax.Precision.HIGHEST)
    return spectra.reshape(sample_rows.shape[0], channels, 2 * spectra_len).astype(jnp.bfloat16)


def correlate(own_rows, columns, spectra_len):
    blocks = columns.shape[2] // (2 * spectra_len)
    shaped = columns.reshape(columns.shape[0], columns.shape[1], blocks, 2, spectra_len)
    rotated = jnp.stack([-shaped[:, :, :, 1, :], shaped[:, :, :, 0, :]], axis=3).reshape(
        columns.shape
    )
    stacked = jnp.concatenate([columns, rotated], axis=0)
    stacked = jnp.transpose(stacked, (1, 0, 2))
    own_first = jnp.transpose(own_rows, (1, 0, 2))
    product = jnp.einsum("cik,cjk->cij", own_first, stacked, preferred_element_type=jnp.float32)
    count = columns.shape[0]
    product = product.reshape(product.shape[0], product.shape[1], 2, count)
    return jnp.transpose(product, (0, 2, 1, 3))


def gathered_shards(voltages, fir_taps):
    samples = voltages[0]
    batch_count = samples.shape[1]
    tap_count, frame = fir_taps.shape
    spectra_len = samples.shape[2] // frame - tap_count + 1
    transform = dft_rows(frame // 2)
    pieces = [
        channelize(samples[:, batch], fir_taps, transform, spectra_len)
        for batch in range(batch_count)
    ]
    spectra = jnp.concatenate(pieces, axis=2)[None]
    turned = lax.all_to_all(spectra, "chan", split_axis=2, concat_axis=1, tiled=True)
    own_rows = turned[0]
    arrived = lax.all_gather(turned, "pair", axis=0, tiled=True)
    flat = arrived.reshape(arrived.shape[0] * arrived.shape[1], arrived.shape[2], arrived.shape[3])
    summed = correlate(own_rows, flat, spectra_len)
    return summed * (1.0 / math.sqrt(batch_count * spectra_len))


def channelize_kernel(antennas, batches, frames, v_ref, taps_ref, dft_ref, o_ref, x_ref, f_ref):
    taps, frame = taps_ref.shape
    parts = frame // LANES
    step = parts * batches
    spectra = frames - taps + 1
    x_ref[...] = v_ref[...].astype(jnp.float32)
    for a in range(antennas):
        for b in range(batches):
            for h in range(parts):
                lanes = slice(h * LANES, (h + 1) * LANES)
                total = None
                for p in range(taps):
                    first = (a * frames + p) * step + h * batches + b
                    term = taps_ref[p : p + 1, lanes] * x_ref[pl.ds(first, spectra, stride=step), :]
                    total = term if total is None else total + term
                f_ref[a, b * spectra : (b + 1) * spectra, lanes] = total.astype(jnp.bfloat16)
        spec = lax.dot_general(
            dft_ref[...], f_ref[a], (((1,), (1,)), ((), ())), preferred_element_type=jnp.float32
        )
        o_ref[:, a, :, :] = spec.astype(jnp.bfloat16).reshape(
            o_ref.shape[0], o_ref.shape[2], o_ref.shape[3]
        )


def correlate_kernel(groups, blocks, antennas, channels, scale, y_ref, *refs):
    outs, scr, vis = refs[: blocks], refs[blocks], refs[blocks + 1]
    rows = antennas * channels * 2
    width = y_ref.shape[1]
    parts = width // LANES
    total = groups * blocks * antennas
    for g in range(groups):
        for q in range(blocks):
            src = y_ref[(g * blocks + q) * rows : (g * blocks + q + 1) * rows, :].astype(jnp.float32)
            for t in range(parts):
                scr[t, (q * groups + g) * rows : (q * groups + g + 1) * rows, :] = src[
                    :, t * LANES : (t + 1) * LANES
                ]
    for c in range(channels):
        re = [scr[t, pl.ds(2 * c, total, stride=2 * channels), :] for t in range(parts)]
        im = [scr[t, pl.ds(2 * c + 1, total, stride=2 * channels), :] for t in range(parts)]
        own = jnp.concatenate(re + im, axis=1).astype(jnp.bfloat16)
        turned = jnp.concatenate([-x for x in im] + re, axis=1).astype(jnp.bfloat16)
        both = jnp.concatenate([own, turned], axis=0)
        prod = lax.dot_general(
            own, both, (((1,), (1,)), ((), ())), preferred_element_type=jnp.float32
        )
        vis[:, c, :, :] = (prod * scale).reshape(blocks, total // blocks, 2 * total)
    me = lax.axis_index("pair")
    for j in range(blocks):
        outs[j][...] = vis[me ^ j]


def place_kernel(blocks, *refs):
    ins, o_ref = refs[:blocks], refs[blocks]
    channels = ins[0].shape[0]
    columns = ins[0].shape[2] // 2
    me = lax.axis_index("pair")
    for j in range(blocks):
        at = pl.ds((me ^ j) * channels, channels)
        block = ins[j][...]
        o_ref[at, 0, :, :] = block[:, :, :columns]
        o_ref[at, 1, :, :] = block[:, :, columns:]


def exchanged_shards(groups, blocks, voltages, fir_taps):
    _, antennas, batches, length = voltages.shape
    taps, frame = fir_taps.shape
    frames = length // frame
    spectra = frames - taps + 1
    parts = frame // LANES
    devices = groups * blocks
    channels = frame // 2 // devices
    total = devices * antennas
    rows = antennas * frames * parts * batches
    lined = voltages.reshape(antennas, batches, frames * parts, LANES)
    lined = jnp.transpose(lined, (0, 2, 1, 3)).reshape(rows, LANES)
    table = jnp.asarray(dft_table(frame // 2), jnp.bfloat16)
    vmem = pl.BlockSpec(memory_space=VMEM)
    sent = pl.pallas_call(
        functools.partial(channelize_kernel, antennas, batches, frames),
        out_shape=jax.ShapeDtypeStruct(
            (devices, antennas, 2 * channels, batches * spectra), jnp.bfloat16
        ),
        in_specs=[vmem] * 3,
        out_specs=vmem,
        scratch_shapes=[
            pltpu.VMEM((rows, LANES), jnp.float32),
            pltpu.VMEM((antennas, batches * spectra, frame), jnp.bfloat16),
        ],
        compiler_params=pltpu.CompilerParams(vmem_limit_bytes=LIMIT),
        name="channelize",
    )(lined, fir_taps, table)
    sent = sent.reshape(devices, antennas * 2 * channels, batches * spectra)
    turned = lax.all_to_all(sent, ("chan", "pair"), 0, 0, tiled=True)
    own_shape = jax.ShapeDtypeStruct((channels, total // blocks, 2 * total), jnp.float32)
    pieces = pl.pallas_call(
        functools.partial(
            correlate_kernel,
            groups,
            blocks,
            antennas,
            channels,
            1.0 / math.sqrt(batches * spectra),
        ),
        out_shape=[own_shape] * blocks,
        in_specs=[vmem],
        out_specs=[vmem] * blocks,
        scratch_shapes=[
            pltpu.VMEM(
                (batches * spectra // LANES, devices * antennas * 2 * channels, LANES), jnp.float32
            ),
            pltpu.VMEM((blocks, channels, total // blocks, 2 * total), jnp.float32),
        ],
        compiler_params=pltpu.CompilerParams(vmem_limit_bytes=LIMIT),
        name="correlate",
    )(turned.reshape(devices * antennas * 2 * channels, batches * spectra))
    arrived = [pieces[0]] + [
        lax.ppermute(pieces[j], "pair", [(i, i ^ j) for i in range(blocks)])
        for j in range(1, blocks)
    ]
    return pl.pallas_call(
        functools.partial(place_kernel, blocks),
        out_shape=jax.ShapeDtypeStruct(
            (blocks * channels, 2, total // blocks, total), jnp.float32
        ),
        in_specs=[vmem] * blocks,
        out_specs=vmem,
        compiler_params=pltpu.CompilerParams(vmem_limit_bytes=LIMIT),
        name="place",
    )(*arrived)


def solution(mesh):
    groups, blocks = mesh.shape["chan"], mesh.shape["pair"]
    in_specs = (P("pair", "chan", None, None), P())
    out_specs = P("chan", None, "pair", None)

    def shards(voltages, fir_taps):
        channels = fir_taps.shape[1] // 2
        spectra = voltages.shape[3] // fir_taps.shape[1] - fir_taps.shape[0] + 1
        if (
            channels % (groups * blocks) == 0
            and blocks & (blocks - 1) == 0
            and fir_taps.shape[1] % LANES == 0
            and spectra % LANES == 0
            and voltages.shape[1] * 2 * channels // (groups * blocks) % 16 == 0
        ):
            return exchanged_shards(groups, blocks, voltages, fir_taps)
        return gathered_shards(voltages, fir_taps)

    return jax.shard_map(shards, mesh=mesh, in_specs=in_specs, out_specs=out_specs, check_vma=False)
```

```python
import functools
import math

import jax
import jax.numpy as jnp
import numpy as np
from jax import lax
from jax.experimental import pallas as pl
from jax.experimental.pallas import tpu as pltpu
from jax.sharding import PartitionSpec as P

LANES = 128
LIMIT = 16 * 2**20
VMEM = pltpu.MemorySpace.VMEM


def dft_rows(channels):
    frame = 2 * channels
    row_index = jnp.arange(2 * channels, dtype=jnp.int32)
    col_index = jnp.arange(frame, dtype=jnp.int32)
    freq_index = row_index // 2
    phases = freq_index[:, None] * col_index[None, :] % frame
    angles = phases.astype(jnp.float32) * (2.0 * math.pi / frame)
    chosen = jnp.where((row_index % 2 == 0)[:, None], jnp.cos(angles), -jnp.sin(angles))
    return chosen * (1.0 / math.sqrt(frame))


def dft_table(channels):
    frame = 2 * channels
    row = np.arange(frame)
    phases = (row // 2)[:, None] * np.arange(frame)[None, :] % frame
    angles = phases * (2.0 * np.pi / frame)
    chosen = np.where((row % 2 == 0)[:, None], np.cos(angles), -np.sin(angles))
    return chosen / np.sqrt(frame)


def channelize(sample_rows, fir_taps, transform, spectra_len):
    tap_count, frame = fir_taps.shape
    channels = frame // 2
    framed = sample_rows.astype(jnp.float32).reshape(
        sample_rows.shape[0], spectra_len + tap_count - 1, frame
    )
    filtered = jnp.zeros((sample_rows.shape[0], spectra_len, frame), jnp.float32)
    for tap in range(tap_count):
        filtered = filtered + fir_taps[tap][None, None, :] * framed[:, tap : tap + spectra_len, :]
    spectra = jnp.einsum("wn,asn->aws", transform, filtered, precision=lax.Precision.HIGHEST)
    return spectra.reshape(sample_rows.shape[0], channels, 2 * spectra_len).astype(jnp.bfloat16)


def correlate(own_rows, columns, spectra_len):
    blocks = columns.shape[2] // (2 * spectra_len)
    shaped = columns.reshape(columns.shape[0], columns.shape[1], blocks, 2, spectra_len)
    rotated = jnp.stack([-shaped[:, :, :, 1, :], shaped[:, :, :, 0, :]], axis=3).reshape(
        columns.shape
    )
    stacked = jnp.concatenate([columns, rotated], axis=0)
    stacked = jnp.transpose(stacked, (1, 0, 2))
    own_first = jnp.transpose(own_rows, (1, 0, 2))
    product = jnp.einsum("cik,cjk->cij", own_first, stacked, preferred_element_type=jnp.float32)
    count = columns.shape[0]
    product = product.reshape(product.shape[0], product.shape[1], 2, count)
    return jnp.transpose(product, (0, 2, 1, 3))


def gathered_shards(voltages, fir_taps):
    samples = voltages[0]
    batch_count = samples.shape[1]
    tap_count, frame = fir_taps.shape
    spectra_len = samples.shape[2] // frame - tap_count + 1
    transform = dft_rows(frame // 2)
    pieces = [
        channelize(samples[:, batch], fir_taps, transform, spectra_len)
        for batch in range(batch_count)
    ]
    spectra = jnp.concatenate(pieces, axis=2)[None]
    turned = lax.all_to_all(spectra, "chan", split_axis=2, concat_axis=1, tiled=True)
    own_rows = turned[0]
    arrived = lax.all_gather(turned, "pair", axis=0, tiled=True)
    flat = arrived.reshape(arrived.shape[0] * arrived.shape[1], arrived.shape[2], arrived.shape[3])
    summed = correlate(own_rows, flat, spectra_len)
    return summed * (1.0 / math.sqrt(batch_count * spectra_len))


def channelize_kernel(v_hbm, taps_hbm, dft_hbm, o_ref, v_ref, taps_ref, dft_ref, x_ref, f_ref, sems):
    antennas, batches, length = v_ref.shape
    taps, frame = taps_ref.shape
    copies = [pltpu.make_async_copy(v_hbm.at[a], v_ref.at[a], sems.at[a]) for a in range(antennas)]
    copy_taps = pltpu.make_async_copy(taps_hbm, taps_ref, sems.at[antennas])
    copy_dft = pltpu.make_async_copy(dft_hbm, dft_ref, sems.at[antennas + 1])
    for copy in [copy_taps] + copies + [copy_dft]:
        copy.start()
    copy_taps.wait()
    parts = frame // LANES
    spectra = length // frame - taps + 1
    for a in range(antennas):
        copies[a].wait()
        samples = v_ref[a].astype(jnp.float32)
        for b in range(batches):
            x_ref[a, b] = samples[b].reshape(length // LANES, LANES)
        for b in range(batches):
            for h in range(parts):
                lanes = slice(h * LANES, (h + 1) * LANES)
                total = None
                for p in range(taps):
                    rows = x_ref[a, b, pl.ds(p * parts + h, spectra, stride=parts), :]
                    term = taps_ref[p : p + 1, lanes] * rows
                    total = term if total is None else total + term
                f_ref[a, b * spectra : (b + 1) * spectra, lanes] = total.astype(jnp.bfloat16)
        if a == 0:
            copy_dft.wait()
        spec = lax.dot_general(
            dft_ref[...], f_ref[a], (((1,), (1,)), ((), ())), preferred_element_type=jnp.float32
        )
        o_ref[:, a, :, :] = spec.astype(jnp.bfloat16).reshape(
            o_ref.shape[0], o_ref.shape[2], o_ref.shape[3]
        )


def correlate_kernel(groups, blocks, antennas, channels, scale, y_ref, *refs):
    outs, scr, vis = refs[: blocks], refs[blocks], refs[blocks + 1]
    rows = antennas * channels * 2
    width = y_ref.shape[1]
    parts = width // LANES
    total = groups * blocks * antennas
    for g in range(groups):
        for q in range(blocks):
            src = y_ref[(g * blocks + q) * rows : (g * blocks + q + 1) * rows, :].astype(jnp.float32)
            for t in range(parts):
                scr[t, (q * groups + g) * rows : (q * groups + g + 1) * rows, :] = src[
                    :, t * LANES : (t + 1) * LANES
                ]
    for c in range(channels):
        re = [scr[t, pl.ds(2 * c, total, stride=2 * channels), :] for t in range(parts)]
        im = [scr[t, pl.ds(2 * c + 1, total, stride=2 * channels), :] for t in range(parts)]
        own = jnp.concatenate(re + im, axis=1).astype(jnp.bfloat16)
        turned = jnp.concatenate([-x for x in im] + re, axis=1).astype(jnp.bfloat16)
        both = jnp.concatenate([own, turned], axis=0)
        prod = lax.dot_general(
            own, both, (((1,), (1,)), ((), ())), preferred_element_type=jnp.float32
        )
        vis[:, c, :, :] = (prod * scale).reshape(blocks, total // blocks, 2 * total)
    me = lax.axis_index("pair")
    for j in range(blocks):
        outs[j][...] = vis[me ^ j]


def place_kernel(blocks, *refs):
    ins, o_ref = refs[:blocks], refs[blocks]
    channels = ins[0].shape[0]
    columns = ins[0].shape[2] // 2
    me = lax.axis_index("pair")
    for j in range(blocks):
        at = pl.ds((me ^ j) * channels, channels)
        block = ins[j][...]
        o_ref[at, 0, :, :] = block[:, :, :columns]
        o_ref[at, 1, :, :] = block[:, :, columns:]


def exchanged_shards(groups, blocks, voltages, fir_taps):
    _, antennas, batches, length = voltages.shape
    taps, frame = fir_taps.shape
    frames = length // frame
    spectra = frames - taps + 1
    devices = groups * blocks
    channels = frame // 2 // devices
    total = devices * antennas
    table = jnp.asarray(dft_table(frame // 2), jnp.bfloat16)
    vmem = pl.BlockSpec(memory_space=VMEM)
    hbm = pl.BlockSpec(memory_space=pltpu.MemorySpace.HBM)
    sent = pl.pallas_call(
        channelize_kernel,
        out_shape=jax.ShapeDtypeStruct(
            (devices, antennas, 2 * channels, batches * spectra), jnp.bfloat16
        ),
        in_specs=[hbm] * 3,
        out_specs=vmem,
        scratch_shapes=[
            pltpu.VMEM((antennas, batches, length), jnp.bfloat16),
            pltpu.VMEM((taps, frame), jnp.float32),
            pltpu.VMEM((frame, frame), jnp.bfloat16),
            pltpu.VMEM((antennas, batches, length // LANES, LANES), jnp.float32),
            pltpu.VMEM((antennas, batches * spectra, frame), jnp.bfloat16),
            pltpu.SemaphoreType.DMA((antennas + 2,)),
        ],
        compiler_params=pltpu.CompilerParams(vmem_limit_bytes=LIMIT),
        name="channelize",
    )(*[pltpu.with_memory_space_constraint(x, pltpu.MemorySpace.HBM) for x in (voltages[0], fir_taps, table)])
    sent = sent.reshape(devices, antennas * 2 * channels, batches * spectra)
    turned = lax.all_to_all(sent, ("chan", "pair"), 0, 0, tiled=True)
    own_shape = jax.ShapeDtypeStruct((channels, total // blocks, 2 * total), jnp.float32)
    pieces = pl.pallas_call(
        functools.partial(
            correlate_kernel,
            groups,
            blocks,
            antennas,
            channels,
            1.0 / math.sqrt(batches * spectra),
        ),
        out_shape=[own_shape] * blocks,
        in_specs=[vmem],
        out_specs=[vmem] * blocks,
        scratch_shapes=[
            pltpu.VMEM(
                (batches * spectra // LANES, devices * antennas * 2 * channels, LANES), jnp.float32
            ),
            pltpu.VMEM((blocks, channels, total // blocks, 2 * total), jnp.float32),
        ],
        compiler_params=pltpu.CompilerParams(vmem_limit_bytes=LIMIT),
        name="correlate",
    )(turned.reshape(devices * antennas * 2 * channels, batches * spectra))
    arrived = [pieces[0]] + [
        lax.ppermute(pieces[j], "pair", [(i, i ^ j) for i in range(blocks)])
        for j in range(1, blocks)
    ]
    return pl.pallas_call(
        functools.partial(place_kernel, blocks),
        out_shape=jax.ShapeDtypeStruct(
            (blocks * channels, 2, total // blocks, total), jnp.float32
        ),
        in_specs=[vmem] * blocks,
        out_specs=vmem,
        compiler_params=pltpu.CompilerParams(vmem_limit_bytes=LIMIT),
        name="place",
    )(*arrived)


def solution(mesh):
    groups, blocks = mesh.shape["chan"], mesh.shape["pair"]
    in_specs = (P("pair", "chan", None, None), P())
    out_specs = P("chan", None, "pair", None)

    def shards(voltages, fir_taps):
        channels = fir_taps.shape[1] // 2
        spectra = voltages.shape[3] // fir_taps.shape[1] - fir_taps.shape[0] + 1
        if (
            channels % (groups * blocks) == 0
            and blocks & (blocks - 1) == 0
            and fir_taps.shape[1] % LANES == 0
            and spectra % LANES == 0
            and voltages.shape[1] * 2 * channels // (groups * blocks) % 16 == 0
        ):
            return exchanged_shards(groups, blocks, voltages, fir_taps)
        return gathered_shards(voltages, fir_taps)

    return jax.shard_map(shards, mesh=mesh, in_specs=in_specs, out_specs=out_specs, check_vma=False)
```

```python
import functools
import math

import jax
import jax.numpy as jnp
import numpy as np
from jax import lax
from jax.experimental import pallas as pl
from jax.experimental.pallas import tpu as pltpu
from jax.sharding import PartitionSpec as P

LANES = 128
LIMIT = 16 * 2**20
VMEM = pltpu.MemorySpace.VMEM


def dft_rows(channels):
    frame = 2 * channels
    row_index = jnp.arange(2 * channels, dtype=jnp.int32)
    col_index = jnp.arange(frame, dtype=jnp.int32)
    freq_index = row_index // 2
    phases = freq_index[:, None] * col_index[None, :] % frame
    angles = phases.astype(jnp.float32) * (2.0 * math.pi / frame)
    chosen = jnp.where((row_index % 2 == 0)[:, None], jnp.cos(angles), -jnp.sin(angles))
    return chosen * (1.0 / math.sqrt(frame))


def dft_table(channels):
    frame = 2 * channels
    row = np.arange(frame)
    phases = (row // 2)[:, None] * np.arange(frame)[None, :] % frame
    angles = phases * (2.0 * np.pi / frame)
    chosen = np.where((row % 2 == 0)[:, None], np.cos(angles), -np.sin(angles))
    return chosen / np.sqrt(frame)


def channelize(sample_rows, fir_taps, transform, spectra_len):
    tap_count, frame = fir_taps.shape
    channels = frame // 2
    framed = sample_rows.astype(jnp.float32).reshape(
        sample_rows.shape[0], spectra_len + tap_count - 1, frame
    )
    filtered = jnp.zeros((sample_rows.shape[0], spectra_len, frame), jnp.float32)
    for tap in range(tap_count):
        filtered = filtered + fir_taps[tap][None, None, :] * framed[:, tap : tap + spectra_len, :]
    spectra = jnp.einsum("wn,asn->aws", transform, filtered, precision=lax.Precision.HIGHEST)
    return spectra.reshape(sample_rows.shape[0], channels, 2 * spectra_len).astype(jnp.bfloat16)


def correlate(own_rows, columns, spectra_len):
    blocks = columns.shape[2] // (2 * spectra_len)
    shaped = columns.reshape(columns.shape[0], columns.shape[1], blocks, 2, spectra_len)
    rotated = jnp.stack([-shaped[:, :, :, 1, :], shaped[:, :, :, 0, :]], axis=3).reshape(
        columns.shape
    )
    stacked = jnp.concatenate([columns, rotated], axis=0)
    stacked = jnp.transpose(stacked, (1, 0, 2))
    own_first = jnp.transpose(own_rows, (1, 0, 2))
    product = jnp.einsum("cik,cjk->cij", own_first, stacked, preferred_element_type=jnp.float32)
    count = columns.shape[0]
    product = product.reshape(product.shape[0], product.shape[1], 2, count)
    return jnp.transpose(product, (0, 2, 1, 3))


def gathered_shards(voltages, fir_taps):
    samples = voltages[0]
    batch_count = samples.shape[1]
    tap_count, frame = fir_taps.shape
    spectra_len = samples.shape[2] // frame - tap_count + 1
    transform = dft_rows(frame // 2)
    pieces = [
        channelize(samples[:, batch], fir_taps, transform, spectra_len)
        for batch in range(batch_count)
    ]
    spectra = jnp.concatenate(pieces, axis=2)[None]
    turned = lax.all_to_all(spectra, "chan", split_axis=2, concat_axis=1, tiled=True)
    own_rows = turned[0]
    arrived = lax.all_gather(turned, "pair", axis=0, tiled=True)
    flat = arrived.reshape(arrived.shape[0] * arrived.shape[1], arrived.shape[2], arrived.shape[3])
    summed = correlate(own_rows, flat, spectra_len)
    return summed * (1.0 / math.sqrt(batch_count * spectra_len))


def channelize_kernel(v_hbm, taps_hbm, dft_hbm, o_ref, v_ref, taps_ref, dft_ref, x_ref, f_ref, sems):
    antennas, batches, length = v_ref.shape
    taps, frame = taps_ref.shape
    copies = [pltpu.make_async_copy(v_hbm.at[a], v_ref.at[a], sems.at[a]) for a in range(antennas)]
    copy_taps = pltpu.make_async_copy(taps_hbm, taps_ref, sems.at[antennas])
    copy_dft = pltpu.make_async_copy(dft_hbm, dft_ref, sems.at[antennas + 1])
    for copy in copies + [copy_taps, copy_dft]:
        copy.start()
    copy_taps.wait()
    parts = frame // LANES
    spectra = length // frame - taps + 1
    for a in range(antennas):
        copies[a].wait()
        samples = v_ref[a].astype(jnp.float32)
        for b in range(batches):
            x_ref[a, b] = samples[b].reshape(length // LANES, LANES)
        for b in range(batches):
            for h in range(parts):
                lanes = slice(h * LANES, (h + 1) * LANES)
                total = None
                for p in range(taps):
                    rows = x_ref[a, b, pl.ds(p * parts + h, spectra, stride=parts), :]
                    term = taps_ref[p : p + 1, lanes] * rows
                    total = term if total is None else total + term
                f_ref[a, b * spectra : (b + 1) * spectra, lanes] = total.astype(jnp.bfloat16)
    copy_dft.wait()
    for a in range(antennas):
        spec = lax.dot_general(
            dft_ref[...], f_ref[a], (((1,), (1,)), ((), ())), preferred_element_type=jnp.float32
        )
        o_ref[:, a, :, :] = spec.astype(jnp.bfloat16).reshape(
            o_ref.shape[0], o_ref.shape[2], o_ref.shape[3]
        )


def correlate_kernel(groups, blocks, antennas, channels, scale, y_ref, *refs):
    outs, scr, vis = refs[: blocks], refs[blocks], refs[blocks + 1]
    rows = antennas * channels * 2
    width = y_ref.shape[1]
    parts = width // LANES
    total = groups * blocks * antennas
    for g in range(groups):
        for q in range(blocks):
            src = y_ref[(g * blocks + q) * rows : (g * blocks + q + 1) * rows, :].astype(jnp.float32)
            for t in range(parts):
                scr[t, (q * groups + g) * rows : (q * groups + g + 1) * rows, :] = src[
                    :, t * LANES : (t + 1) * LANES
                ]
    for c in range(channels):
        re = [scr[t, pl.ds(2 * c, total, stride=2 * channels), :] for t in range(parts)]
        im = [scr[t, pl.ds(2 * c + 1, total, stride=2 * channels), :] for t in range(parts)]
        own = jnp.concatenate(re + im, axis=1).astype(jnp.bfloat16)
        turned = jnp.concatenate([-x for x in im] + re, axis=1).astype(jnp.bfloat16)
        both = jnp.concatenate([own, turned], axis=0)
        prod = lax.dot_general(
            own, both, (((1,), (1,)), ((), ())), preferred_element_type=jnp.float32
        )
        vis[:, c, :, :] = (prod * scale).reshape(blocks, total // blocks, 2 * total)
    me = lax.axis_index("pair")
    for j in range(blocks):
        outs[j][...] = vis[me ^ j].astype(outs[j].dtype)


def place_kernel(blocks, *refs):
    ins, o_ref = refs[:blocks], refs[blocks]
    channels = ins[0].shape[0]
    columns = ins[0].shape[2] // 2
    me = lax.axis_index("pair")
    for j in range(blocks):
        at = pl.ds((me ^ j) * channels, channels)
        block = ins[j][...].astype(jnp.float32)
        o_ref[at, 0, :, :] = block[:, :, :columns]
        o_ref[at, 1, :, :] = block[:, :, columns:]


def exchanged_shards(groups, blocks, voltages, fir_taps):
    _, antennas, batches, length = voltages.shape
    taps, frame = fir_taps.shape
    frames = length // frame
    spectra = frames - taps + 1
    devices = groups * blocks
    channels = frame // 2 // devices
    total = devices * antennas
    table = jnp.asarray(dft_table(frame // 2), jnp.bfloat16)
    vmem = pl.BlockSpec(memory_space=VMEM)
    hbm = pl.BlockSpec(memory_space=pltpu.MemorySpace.HBM)
    sent = pl.pallas_call(
        channelize_kernel,
        out_shape=jax.ShapeDtypeStruct(
            (devices, antennas, 2 * channels, batches * spectra), jnp.bfloat16
        ),
        in_specs=[hbm] * 3,
        out_specs=vmem,
        scratch_shapes=[
            pltpu.VMEM((antennas, batches, length), jnp.bfloat16),
            pltpu.VMEM((taps, frame), jnp.float32),
            pltpu.VMEM((frame, frame), jnp.bfloat16),
            pltpu.VMEM((antennas, batches, length // LANES, LANES), jnp.float32),
            pltpu.VMEM((antennas, batches * spectra, frame), jnp.bfloat16),
            pltpu.SemaphoreType.DMA((antennas + 2,)),
        ],
        compiler_params=pltpu.CompilerParams(vmem_limit_bytes=LIMIT),
        name="channelize",
    )(*[pltpu.with_memory_space_constraint(x, pltpu.MemorySpace.HBM) for x in (voltages[0], fir_taps, table)])
    sent = sent.reshape(devices, antennas * 2 * channels, batches * spectra)
    turned = lax.all_to_all(sent, ("chan", "pair"), 0, 0, tiled=True)
    piece = (channels, total // blocks, 2 * total)
    kinds = [jnp.float32 if j < 2 else jnp.bfloat16 for j in range(blocks)]
    pieces = pl.pallas_call(
        functools.partial(
            correlate_kernel,
            groups,
            blocks,
            antennas,
            channels,
            1.0 / math.sqrt(batches * spectra),
        ),
        out_shape=[jax.ShapeDtypeStruct(piece, kind) for kind in kinds],
        in_specs=[vmem],
        out_specs=[vmem] * blocks,
        scratch_shapes=[
            pltpu.VMEM(
                (batches * spectra // LANES, devices * antennas * 2 * channels, LANES), jnp.float32
            ),
            pltpu.VMEM((blocks, channels, total // blocks, 2 * total), jnp.float32),
        ],
        compiler_params=pltpu.CompilerParams(vmem_limit_bytes=LIMIT),
        name="correlate",
    )(turned.reshape(devices * antennas * 2 * channels, batches * spectra))
    arrived = [pieces[0]] + [
        lax.ppermute(pieces[j], "pair", [(i, i ^ j) for i in range(blocks)])
        for j in range(1, blocks)
    ]
    return pl.pallas_call(
        functools.partial(place_kernel, blocks),
        out_shape=jax.ShapeDtypeStruct(
            (blocks * channels, 2, total // blocks, total), jnp.float32
        ),
        in_specs=[vmem] * blocks,
        out_specs=vmem,
        compiler_params=pltpu.CompilerParams(vmem_limit_bytes=LIMIT),
        name="place",
    )(*arrived)


def solution(mesh):
    groups, blocks = mesh.shape["chan"], mesh.shape["pair"]
    in_specs = (P("pair", "chan", None, None), P())
    out_specs = P("chan", None, "pair", None)

    def shards(voltages, fir_taps):
        channels = fir_taps.shape[1] // 2
        spectra = voltages.shape[3] // fir_taps.shape[1] - fir_taps.shape[0] + 1
        if (
            channels % (groups * blocks) == 0
            and blocks & (blocks - 1) == 0
            and fir_taps.shape[1] % LANES == 0
            and spectra % LANES == 0
            and voltages.shape[1] * 2 * channels // (groups * blocks) % 16 == 0
        ):
            return exchanged_shards(groups, blocks, voltages, fir_taps)
        return gathered_shards(voltages, fir_taps)

    return jax.shard_map(shards, mesh=mesh, in_specs=in_specs, out_specs=out_specs, check_vma=False)
```

```python
import functools
import math

import jax
import jax.numpy as jnp
import numpy as np
from jax import lax
from jax.experimental import pallas as pl
from jax.experimental.pallas import tpu as pltpu
from jax.sharding import PartitionSpec as P

LANES = 128
LIMIT = 16 * 2**20
VMEM = pltpu.MemorySpace.VMEM


def dft_rows(channels):
    frame = 2 * channels
    row_index = jnp.arange(2 * channels, dtype=jnp.int32)
    col_index = jnp.arange(frame, dtype=jnp.int32)
    freq_index = row_index // 2
    phases = freq_index[:, None] * col_index[None, :] % frame
    angles = phases.astype(jnp.float32) * (2.0 * math.pi / frame)
    chosen = jnp.where((row_index % 2 == 0)[:, None], jnp.cos(angles), -jnp.sin(angles))
    return chosen * (1.0 / math.sqrt(frame))


def dft_table(channels):
    frame = 2 * channels
    row = np.arange(frame)
    phases = (row // 2)[:, None] * np.arange(frame)[None, :] % frame
    angles = phases * (2.0 * np.pi / frame)
    chosen = np.where((row % 2 == 0)[:, None], np.cos(angles), -np.sin(angles))
    return chosen / np.sqrt(frame)


def channelize(sample_rows, fir_taps, transform, spectra_len):
    tap_count, frame = fir_taps.shape
    channels = frame // 2
    framed = sample_rows.astype(jnp.float32).reshape(
        sample_rows.shape[0], spectra_len + tap_count - 1, frame
    )
    filtered = jnp.zeros((sample_rows.shape[0], spectra_len, frame), jnp.float32)
    for tap in range(tap_count):
        filtered = filtered + fir_taps[tap][None, None, :] * framed[:, tap : tap + spectra_len, :]
    spectra = jnp.einsum("wn,asn->aws", transform, filtered, precision=lax.Precision.HIGHEST)
    return spectra.reshape(sample_rows.shape[0], channels, 2 * spectra_len).astype(jnp.bfloat16)


def correlate(own_rows, columns, spectra_len):
    blocks = columns.shape[2] // (2 * spectra_len)
    shaped = columns.reshape(columns.shape[0], columns.shape[1], blocks, 2, spectra_len)
    rotated = jnp.stack([-shaped[:, :, :, 1, :], shaped[:, :, :, 0, :]], axis=3).reshape(
        columns.shape
    )
    stacked = jnp.concatenate([columns, rotated], axis=0)
    stacked = jnp.transpose(stacked, (1, 0, 2))
    own_first = jnp.transpose(own_rows, (1, 0, 2))
    product = jnp.einsum("cik,cjk->cij", own_first, stacked, preferred_element_type=jnp.float32)
    count = columns.shape[0]
    product = product.reshape(product.shape[0], product.shape[1], 2, count)
    return jnp.transpose(product, (0, 2, 1, 3))


def gathered_shards(voltages, fir_taps):
    samples = voltages[0]
    batch_count = samples.shape[1]
    tap_count, frame = fir_taps.shape
    spectra_len = samples.shape[2] // frame - tap_count + 1
    transform = dft_rows(frame // 2)
    pieces = [
        channelize(samples[:, batch], fir_taps, transform, spectra_len)
        for batch in range(batch_count)
    ]
    spectra = jnp.concatenate(pieces, axis=2)[None]
    turned = lax.all_to_all(spectra, "chan", split_axis=2, concat_axis=1, tiled=True)
    own_rows = turned[0]
    arrived = lax.all_gather(turned, "pair", axis=0, tiled=True)
    flat = arrived.reshape(arrived.shape[0] * arrived.shape[1], arrived.shape[2], arrived.shape[3])
    summed = correlate(own_rows, flat, spectra_len)
    return summed * (1.0 / math.sqrt(batch_count * spectra_len))


def times_transposed(left, right):
    return lax.dot_general(
        left, right, (((1,), (1,)), ((), ())), preferred_element_type=jnp.float32
    )


def channelize_kernel(v_hbm, taps_hbm, dft_hbm, o_ref, v_ref, taps_ref, dft_ref, x_ref, f_ref, sems):
    antennas, batches, length = v_ref.shape
    taps, frame = taps_ref.shape
    copies = [pltpu.make_async_copy(v_hbm.at[a], v_ref.at[a], sems.at[a]) for a in range(antennas)]
    copy_taps = pltpu.make_async_copy(taps_hbm, taps_ref, sems.at[antennas])
    copy_dft = pltpu.make_async_copy(dft_hbm, dft_ref, sems.at[antennas + 1])
    for copy in copies + [copy_taps, copy_dft]:
        copy.start()
    copy_taps.wait()
    parts = frame // LANES
    spectra = length // frame - taps + 1
    for a in range(antennas):
        copies[a].wait()
        samples = v_ref[a].astype(jnp.float32)
        for b in range(batches):
            x_ref[a, b] = samples[b].reshape(length // LANES, LANES)
        for b in range(batches):
            for h in range(parts):
                lanes = slice(h * LANES, (h + 1) * LANES)
                total = None
                for p in range(taps):
                    rows = x_ref[a, b, pl.ds(p * parts + h, spectra, stride=parts), :]
                    term = taps_ref[p : p + 1, lanes] * rows
                    total = term if total is None else total + term
                high = total.astype(jnp.bfloat16)
                times = slice(b * spectra, (b + 1) * spectra)
                f_ref[0, a, times, lanes] = high
                f_ref[1, a, times, lanes] = (total - high.astype(jnp.float32)).astype(jnp.bfloat16)
    copy_dft.wait()
    for a in range(antennas):
        spec = times_transposed(dft_ref[0], f_ref[0, a])
        spec = spec + times_transposed(dft_ref[1], f_ref[0, a])
        spec = spec + times_transposed(dft_ref[0], f_ref[1, a])
        o_ref[:, a, :, :] = spec.astype(jnp.bfloat16).reshape(
            o_ref.shape[0], o_ref.shape[2], o_ref.shape[3]
        )


def correlate_kernel(groups, blocks, antennas, channels, scale, y_ref, *refs):
    outs, scr, vis = refs[: blocks], refs[blocks], refs[blocks + 1]
    rows = antennas * channels * 2
    width = y_ref.shape[1]
    parts = width // LANES
    total = groups * blocks * antennas
    for g in range(groups):
        for q in range(blocks):
            src = y_ref[(g * blocks + q) * rows : (g * blocks + q + 1) * rows, :].astype(jnp.float32)
            for t in range(parts):
                scr[t, (q * groups + g) * rows : (q * groups + g + 1) * rows, :] = src[
                    :, t * LANES : (t + 1) * LANES
                ]
    for c in range(channels):
        re = [scr[t, pl.ds(2 * c, total, stride=2 * channels), :] for t in range(parts)]
        im = [scr[t, pl.ds(2 * c + 1, total, stride=2 * channels), :] for t in range(parts)]
        own = jnp.concatenate(re + im, axis=1).astype(jnp.bfloat16)
        turned = jnp.concatenate([-x for x in im] + re, axis=1).astype(jnp.bfloat16)
        both = jnp.concatenate([own, turned], axis=0)
        prod = times_transposed(own, both)
        vis[:, c, :, :] = (prod * scale).reshape(blocks, total // blocks, 2 * total)
    me = lax.axis_index("pair")
    for j in range(blocks):
        outs[j][...] = vis[me ^ j].astype(outs[j].dtype)


def place_kernel(blocks, *refs):
    ins, o_ref = refs[:blocks], refs[blocks]
    channels = ins[0].shape[0]
    columns = ins[0].shape[2] // 2
    me = lax.axis_index("pair")
    for j in range(blocks):
        at = pl.ds((me ^ j) * channels, channels)
        block = ins[j][...].astype(jnp.float32)
        o_ref[at, 0, :, :] = block[:, :, :columns]
        o_ref[at, 1, :, :] = block[:, :, columns:]


def exchanged_shards(groups, blocks, voltages, fir_taps):
    _, antennas, batches, length = voltages.shape
    taps, frame = fir_taps.shape
    frames = length // frame
    spectra = frames - taps + 1
    devices = groups * blocks
    channels = frame // 2 // devices
    total = devices * antennas
    table = dft_table(frame // 2)
    high = table.astype(jnp.bfloat16)
    table = jnp.asarray(np.stack([high, (table - high.astype(np.float64)).astype(jnp.bfloat16)]))
    vmem = pl.BlockSpec(memory_space=VMEM)
    hbm = pl.BlockSpec(memory_space=pltpu.MemorySpace.HBM)
    sent = pl.pallas_call(
        channelize_kernel,
        out_shape=jax.ShapeDtypeStruct(
            (devices, antennas, 2 * channels, batches * spectra), jnp.bfloat16
        ),
        in_specs=[hbm] * 3,
        out_specs=vmem,
        scratch_shapes=[
            pltpu.VMEM((antennas, batches, length), jnp.bfloat16),
            pltpu.VMEM((taps, frame), jnp.float32),
            pltpu.VMEM((2, frame, frame), jnp.bfloat16),
            pltpu.VMEM((antennas, batches, length // LANES, LANES), jnp.float32),
            pltpu.VMEM((2, antennas, batches * spectra, frame), jnp.bfloat16),
            pltpu.SemaphoreType.DMA((antennas + 2,)),
        ],
        compiler_params=pltpu.CompilerParams(vmem_limit_bytes=LIMIT),
        name="channelize",
    )(*[pltpu.with_memory_space_constraint(x, pltpu.MemorySpace.HBM) for x in (voltages[0], fir_taps, table)])
    sent = sent.reshape(devices, antennas * 2 * channels, batches * spectra)
    turned = lax.all_to_all(sent, ("chan", "pair"), 0, 0, tiled=True)
    piece = (channels, total // blocks, 2 * total)
    kinds = [jnp.float32 if j < 2 else jnp.bfloat16 for j in range(blocks)]
    pieces = pl.pallas_call(
        functools.partial(
            correlate_kernel,
            groups,
            blocks,
            antennas,
            channels,
            1.0 / math.sqrt(batches * spectra),
        ),
        out_shape=[jax.ShapeDtypeStruct(piece, kind) for kind in kinds],
        in_specs=[vmem],
        out_specs=[vmem] * blocks,
        scratch_shapes=[
            pltpu.VMEM(
                (batches * spectra // LANES, devices * antennas * 2 * channels, LANES), jnp.float32
            ),
            pltpu.VMEM((blocks, channels, total // blocks, 2 * total), jnp.float32),
        ],
        compiler_params=pltpu.CompilerParams(vmem_limit_bytes=LIMIT),
        name="correlate",
    )(turned.reshape(devices * antennas * 2 * channels, batches * spectra))
    arrived = [pieces[0]] + [
        lax.ppermute(pieces[j], "pair", [(i, i ^ j) for i in range(blocks)])
        for j in range(1, blocks)
    ]
    return pl.pallas_call(
        functools.partial(place_kernel, blocks),
        out_shape=jax.ShapeDtypeStruct(
            (blocks * channels, 2, total // blocks, total), jnp.float32
        ),
        in_specs=[vmem] * blocks,
        out_specs=vmem,
        compiler_params=pltpu.CompilerParams(vmem_limit_bytes=LIMIT),
        name="place",
    )(*arrived)


def solution(mesh):
    groups, blocks = mesh.shape["chan"], mesh.shape["pair"]
    in_specs = (P("pair", "chan", None, None), P())
    out_specs = P("chan", None, "pair", None)

    def shards(voltages, fir_taps):
        channels = fir_taps.shape[1] // 2
        spectra = voltages.shape[3] // fir_taps.shape[1] - fir_taps.shape[0] + 1
        if (
            channels % (groups * blocks) == 0
            and blocks & (blocks - 1) == 0
            and fir_taps.shape[1] % LANES == 0
            and spectra % LANES == 0
            and voltages.shape[1] * 2 * channels // (groups * blocks) % 16 == 0
        ):
            return exchanged_shards(groups, blocks, voltages, fir_taps)
        return gathered_shards(voltages, fir_taps)

    return jax.shard_map(shards, mesh=mesh, in_specs=in_specs, out_specs=out_specs, check_vma=False)
```

```python
import functools
import math

import jax
import jax.numpy as jnp
import numpy as np
from jax import lax
from jax.experimental import pallas as pl
from jax.experimental.pallas import tpu as pltpu
from jax.sharding import PartitionSpec as P


LANES = 128
LIMIT = 16 * 2**20
VMEM = pltpu.MemorySpace.VMEM


def dft_rows(channels):
    frame = 2 * channels
    row_index = jnp.arange(2 * channels, dtype=jnp.int32)
    col_index = jnp.arange(frame, dtype=jnp.int32)
    freq_index = row_index // 2
    phases = freq_index[:, None] * col_index[None, :] % frame
    angles = phases.astype(jnp.float32) * (2.0 * math.pi / frame)
    chosen = jnp.where((row_index % 2 == 0)[:, None], jnp.cos(angles), -jnp.sin(angles))
    return chosen * (1.0 / math.sqrt(frame))


def dft_table(channels):
    frame = 2 * channels
    row = np.arange(frame)
    phases = (row // 2)[:, None] * np.arange(frame)[None, :] % frame
    angles = phases * (2.0 * np.pi / frame)
    chosen = np.where((row % 2 == 0)[:, None], np.cos(angles), -np.sin(angles))
    return chosen / np.sqrt(frame)


def channelize(sample_rows, fir_taps, transform, spectra_len):
    tap_count, frame = fir_taps.shape
    channels = frame // 2
    framed = sample_rows.astype(jnp.float32).reshape(
        sample_rows.shape[0], spectra_len + tap_count - 1, frame
    )
    filtered = jnp.zeros((sample_rows.shape[0], spectra_len, frame), jnp.float32)
    for tap in range(tap_count):
        filtered = filtered + fir_taps[tap][None, None, :] * framed[:, tap : tap + spectra_len, :]
    spectra = jnp.einsum("wn,asn->aws", transform, filtered, precision=lax.Precision.HIGHEST)
    return spectra.reshape(sample_rows.shape[0], channels, 2 * spectra_len).astype(jnp.bfloat16)


def correlate(own_rows, columns, spectra_len):
    blocks = columns.shape[2] // (2 * spectra_len)
    shaped = columns.reshape(columns.shape[0], columns.shape[1], blocks, 2, spectra_len)
    rotated = jnp.stack([-shaped[:, :, :, 1, :], shaped[:, :, :, 0, :]], axis=3).reshape(
        columns.shape
    )
    stacked = jnp.concatenate([columns, rotated], axis=0)
    stacked = jnp.transpose(stacked, (1, 0, 2))
    own_first = jnp.transpose(own_rows, (1, 0, 2))
    product = jnp.einsum("cik,cjk->cij", own_first, stacked, preferred_element_type=jnp.float32)
    count = columns.shape[0]
    product = product.reshape(product.shape[0], product.shape[1], 2, count)
    return jnp.transpose(product, (0, 2, 1, 3))


def gathered_shards(voltages, fir_taps):
    samples = voltages[0]
    batch_count = samples.shape[1]
    tap_count, frame = fir_taps.shape
    spectra_len = samples.shape[2] // frame - tap_count + 1
    transform = dft_rows(frame // 2)
    pieces = [
        channelize(samples[:, batch], fir_taps, transform, spectra_len)
        for batch in range(batch_count)
    ]
    spectra = jnp.concatenate(pieces, axis=2)[None]
    turned = lax.all_to_all(spectra, "chan", split_axis=2, concat_axis=1, tiled=True)
    own_rows = turned[0]
    arrived = lax.all_gather(turned, "pair", axis=0, tiled=True)
    flat = arrived.reshape(arrived.shape[0] * arrived.shape[1], arrived.shape[2], arrived.shape[3])
    summed = correlate(own_rows, flat, spectra_len)
    return summed * (1.0 / math.sqrt(batch_count * spectra_len))


def times_transposed(left, right):
    return lax.dot_general(
        left, right, (((1,), (1,)), ((), ())), preferred_element_type=jnp.float32
    )


def channelize_kernel(v_hbm, taps_hbm, dft_hbm, o_ref, v_ref, taps_ref, dft_ref, x_ref, f_ref, sems):
    antennas, batches, length = v_ref.shape
    taps, frame = taps_ref.shape
    copies = [pltpu.make_async_copy(v_hbm.at[a], v_ref.at[a], sems.at[a]) for a in range(antennas)]
    copy_taps = pltpu.make_async_copy(taps_hbm, taps_ref, sems.at[antennas])
    copy_dft = pltpu.make_async_copy(dft_hbm, dft_ref, sems.at[antennas + 1])
    for copy in copies + [copy_taps, copy_dft]:
        copy.start()
    copy_taps.wait()
    parts = frame // LANES
    spectra = length // frame - taps + 1
    for a in range(antennas):
        copies[a].wait()
        samples = v_ref[a].astype(jnp.float32)
        for b in range(batches):
            x_ref[a, b] = samples[b].reshape(length // LANES, LANES)
        for b in range(batches):
            for h in range(parts):
                lanes = slice(h * LANES, (h + 1) * LANES)
                total = None
                for p in range(taps):
                    rows = x_ref[a, b, pl.ds(p * parts + h, spectra, stride=parts), :]
                    term = taps_ref[p : p + 1, lanes] * rows
                    total = term if total is None else total + term
                high = total.astype(jnp.bfloat16)
                times = slice(b * spectra, (b + 1) * spectra)
                f_ref[0, a, times, lanes] = high
                f_ref[1, a, times, lanes] = (total - high.astype(jnp.float32)).astype(jnp.bfloat16)
    copy_dft.wait()
    for a in range(antennas):
        spec = times_transposed(dft_ref[0], f_ref[0, a])
        spec = spec + times_transposed(dft_ref[1], f_ref[0, a])
        spec = spec + times_transposed(dft_ref[0], f_ref[1, a])
        o_ref[:, a, :, :] = spec.astype(jnp.bfloat16).reshape(
            o_ref.shape[0], o_ref.shape[2], o_ref.shape[3]
        )


def correlate_kernel(groups, blocks, antennas, channels, scale, y_ref, *refs):
    outs, scr, vis = refs[: blocks], refs[blocks], refs[blocks + 1]
    rows = antennas * channels * 2
    width = y_ref.shape[1]
    parts = width // LANES
    total = groups * blocks * antennas
    for g in range(groups):
        for q in range(blocks):
            src = y_ref[(g * blocks + q) * rows : (g * blocks + q + 1) * rows, :].astype(jnp.float32)
            for t in range(parts):
                scr[t, (q * groups + g) * rows : (q * groups + g + 1) * rows, :] = src[
                    :, t * LANES : (t + 1) * LANES
                ]
    for c in range(channels):
        re = [scr[t, pl.ds(2 * c, total, stride=2 * channels), :] for t in range(parts)]
        im = [scr[t, pl.ds(2 * c + 1, total, stride=2 * channels), :] for t in range(parts)]
        own = jnp.concatenate(re + im, axis=1).astype(jnp.bfloat16)
        turned = jnp.concatenate([-x for x in im] + re, axis=1).astype(jnp.bfloat16)
        both = jnp.concatenate([own, turned], axis=0)
        prod = times_transposed(own, both)
        vis[:, c, :, :] = (prod * scale).reshape(blocks, total // blocks, 2 * total)
    me = lax.axis_index("pair")
    for j in range(blocks):
        outs[j][...] = vis[me ^ j].astype(outs[j].dtype)


def place_kernel(blocks, *refs):
    ins, o_ref = refs[:blocks], refs[blocks]
    channels = ins[0].shape[0]
    columns = ins[0].shape[2] // 2
    me = lax.axis_index("pair")
    for j in range(blocks):
        at = pl.ds((me ^ j) * channels, channels)
        block = ins[j][...].astype(jnp.float32)
        o_ref[at, 0, :, :] = block[:, :, :columns]
        o_ref[at, 1, :, :] = block[:, :, columns:]


def exchanged_shards(groups, blocks, voltages, fir_taps):
    _, antennas, batches, length = voltages.shape
    taps, frame = fir_taps.shape
    frames = length // frame
    spectra = frames - taps + 1
    devices = groups * blocks
    channels = frame // 2 // devices
    total = devices * antennas
    table = dft_table(frame // 2)
    high = table.astype(jnp.bfloat16)
    table = jnp.asarray(np.stack([high, (table - high.astype(np.float64)).astype(jnp.bfloat16)]))
    vmem = pl.BlockSpec(memory_space=VMEM)
    hbm = pl.BlockSpec(memory_space=pltpu.MemorySpace.HBM)
    sent = pl.pallas_call(
        channelize_kernel,
        out_shape=jax.ShapeDtypeStruct(
            (devices, antennas, 2 * channels, batches * spectra), jnp.bfloat16
        ),
        in_specs=[hbm] * 3,
        out_specs=vmem,
        scratch_shapes=[
            pltpu.VMEM((antennas, batches, length), jnp.bfloat16),
            pltpu.VMEM((taps, frame), jnp.float32),
            pltpu.VMEM((2, frame, frame), jnp.bfloat16),
            pltpu.VMEM((antennas, batches, length // LANES, LANES), jnp.float32),
            pltpu.VMEM((2, antennas, batches * spectra, frame), jnp.bfloat16),
            pltpu.SemaphoreType.DMA((antennas + 2,)),
        ],
        compiler_params=pltpu.CompilerParams(vmem_limit_bytes=LIMIT),
        name="channelize",
    )(*[pltpu.with_memory_space_constraint(x, pltpu.MemorySpace.HBM) for x in (voltages[0], fir_taps, table)])
    sent = sent.reshape(devices, antennas * 2 * channels, batches * spectra)
    turned = lax.all_to_all(sent, ("chan", "pair"), 0, 0, tiled=True)
    piece = (channels, total // blocks, 2 * total)
    kinds = [jnp.float32 if j < 2 else jnp.bfloat16 for j in range(blocks)]
    pieces = pl.pallas_call(
        functools.partial(
            correlate_kernel,
            groups,
            blocks,
            antennas,
            channels,
            1.0 / math.sqrt(batches * spectra),
        ),
        out_shape=[jax.ShapeDtypeStruct(piece, kind) for kind in kinds],
        in_specs=[vmem],
        out_specs=[vmem] * blocks,
        scratch_shapes=[
            pltpu.VMEM(
                (batches * spectra // LANES, devices * antennas * 2 * channels, LANES), jnp.float32
            ),
            pltpu.VMEM((blocks, channels, total // blocks, 2 * total), jnp.float32),
        ],
        compiler_params=pltpu.CompilerParams(vmem_limit_bytes=LIMIT),
        name="correlate",
    )(turned.reshape(devices * antennas * 2 * channels, batches * spectra))
    arrived = [pieces[0]]
    for j in range(1, blocks):
        arrived.append(
            lax.ppermute(pieces[j], "pair", [(i, i ^ j) for i in range(blocks)])
        )
    return pl.pallas_call(
        functools.partial(place_kernel, blocks),
        out_shape=jax.ShapeDtypeStruct(
            (blocks * channels, 2, total // blocks, total), jnp.float32
        ),
        in_specs=[vmem] * blocks,
        out_specs=vmem,
        compiler_params=pltpu.CompilerParams(vmem_limit_bytes=LIMIT),
        name="place",
    )(*arrived)


def solution(mesh):
    groups, blocks = mesh.shape["chan"], mesh.shape["pair"]
    in_specs = (P("pair", "chan", None, None), P())
    out_specs = P("chan", None, "pair", None)

    def shards(voltages, fir_taps):
        channels = fir_taps.shape[1] // 2
        spectra = voltages.shape[3] // fir_taps.shape[1] - fir_taps.shape[0] + 1
        if (
            channels % (groups * blocks) == 0
            and blocks & (blocks - 1) == 0
            and fir_taps.shape[1] % LANES == 0
            and spectra % LANES == 0
            and voltages.shape[1] * 2 * channels // (groups * blocks) % 16 == 0
        ):
            return exchanged_shards(groups, blocks, voltages, fir_taps)
        return gathered_shards(voltages, fir_taps)

    return jax.shard_map(shards, mesh=mesh, in_specs=in_specs, out_specs=out_specs, check_vma=False)
```

```python
import functools
import math

import jax
import jax.numpy as jnp
import numpy as np
from jax import lax
from jax.experimental import pallas as pl
from jax.experimental.pallas import tpu as pltpu
from jax.sharding import PartitionSpec as P


LANES = 128
LIMIT = 16 * 2**20
VMEM = pltpu.MemorySpace.VMEM


def dft_rows(channels):
    frame = 2 * channels
    row_index = jnp.arange(2 * channels, dtype=jnp.int32)
    col_index = jnp.arange(frame, dtype=jnp.int32)
    freq_index = row_index // 2
    phases = freq_index[:, None] * col_index[None, :] % frame
    angles = phases.astype(jnp.float32) * (2.0 * math.pi / frame)
    chosen = jnp.where((row_index % 2 == 0)[:, None], jnp.cos(angles), -jnp.sin(angles))
    return chosen * (1.0 / math.sqrt(frame))


def dft_table(channels):
    frame = 2 * channels
    row = np.arange(frame)
    phases = (row // 2)[:, None] * np.arange(frame)[None, :] % frame
    angles = phases * (2.0 * np.pi / frame)
    chosen = np.where((row % 2 == 0)[:, None], np.cos(angles), -np.sin(angles))
    return chosen / np.sqrt(frame)


def channelize(sample_rows, fir_taps, transform, spectra_len):
    tap_count, frame = fir_taps.shape
    channels = frame // 2
    framed = sample_rows.astype(jnp.float32).reshape(
        sample_rows.shape[0], spectra_len + tap_count - 1, frame
    )
    filtered = jnp.zeros((sample_rows.shape[0], spectra_len, frame), jnp.float32)
    for tap in range(tap_count):
        filtered = filtered + fir_taps[tap][None, None, :] * framed[:, tap : tap + spectra_len, :]
    spectra = jnp.einsum("wn,asn->aws", transform, filtered, precision=lax.Precision.HIGHEST)
    return spectra.reshape(sample_rows.shape[0], channels, 2 * spectra_len).astype(jnp.bfloat16)


def correlate(own_rows, columns, spectra_len):
    blocks = columns.shape[2] // (2 * spectra_len)
    shaped = columns.reshape(columns.shape[0], columns.shape[1], blocks, 2, spectra_len)
    rotated = jnp.stack([-shaped[:, :, :, 1, :], shaped[:, :, :, 0, :]], axis=3).reshape(
        columns.shape
    )
    stacked = jnp.concatenate([columns, rotated], axis=0)
    stacked = jnp.transpose(stacked, (1, 0, 2))
    own_first = jnp.transpose(own_rows, (1, 0, 2))
    product = jnp.einsum("cik,cjk->cij", own_first, stacked, preferred_element_type=jnp.float32)
    count = columns.shape[0]
    product = product.reshape(product.shape[0], product.shape[1], 2, count)
    return jnp.transpose(product, (0, 2, 1, 3))


def gathered_shards(voltages, fir_taps):
    samples = voltages[0]
    batch_count = samples.shape[1]
    tap_count, frame = fir_taps.shape
    spectra_len = samples.shape[2] // frame - tap_count + 1
    transform = dft_rows(frame // 2)
    pieces = [
        channelize(samples[:, batch], fir_taps, transform, spectra_len)
        for batch in range(batch_count)
    ]
    spectra = jnp.concatenate(pieces, axis=2)[None]
    turned = lax.all_to_all(spectra, "chan", split_axis=2, concat_axis=1, tiled=True)
    own_rows = turned[0]
    arrived = lax.all_gather(turned, "pair", axis=0, tiled=True)
    flat = arrived.reshape(arrived.shape[0] * arrived.shape[1], arrived.shape[2], arrived.shape[3])
    summed = correlate(own_rows, flat, spectra_len)
    return summed * (1.0 / math.sqrt(batch_count * spectra_len))


def times_transposed(left, right):
    return lax.dot_general(
        left, right, (((1,), (1,)), ((), ())), preferred_element_type=jnp.float32
    )


def transformed(dft_ref, high, low):
    total = times_transposed(dft_ref[0], high) + times_transposed(dft_ref[1], high)
    return total + times_transposed(dft_ref[0], low)


def channelize_kernel(v_hbm, taps_hbm, dft_hbm, o_ref, v_ref, taps_ref, dft_ref, x_ref, sems):
    antennas, batches, length = v_ref.shape
    taps, frame = taps_ref.shape
    copies = [pltpu.make_async_copy(v_hbm.at[a], v_ref.at[a], sems.at[a]) for a in range(antennas)]
    copy_taps = pltpu.make_async_copy(taps_hbm, taps_ref, sems.at[antennas])
    copy_dft = pltpu.make_async_copy(dft_hbm, dft_ref, sems.at[antennas + 1])
    for copy in copies + [copy_taps, copy_dft]:
        copy.start()
    copy_taps.wait()
    parts = frame // LANES
    spectra = length // frame - taps + 1
    spec = []
    for a in range(antennas):
        copies[a].wait()
        if a == 1 or antennas == 1:
            copy_dft.wait()
        if a > 0:
            spec.append(transformed(dft_ref, *split))
        samples = v_ref[a].astype(jnp.float32)
        for b in range(batches):
            x_ref[a, b] = samples[b].reshape(length // LANES, LANES)
        filtered = []
        for b in range(batches):
            row = []
            for h in range(parts):
                lanes = slice(h * LANES, (h + 1) * LANES)
                total = None
                for p in range(taps):
                    rows = x_ref[a, b, pl.ds(p * parts + h, spectra, stride=parts), :]
                    term = taps_ref[p : p + 1, lanes] * rows
                    total = term if total is None else total + term
                high = total.astype(jnp.bfloat16)
                row.append((high, (total - high.astype(jnp.float32)).astype(jnp.bfloat16)))
            filtered.append(row)
        split = [
            jnp.concatenate([jnp.concatenate([x[n] for x in row], axis=1) for row in filtered], axis=0)
            for n in range(2)
        ]
    spec.append(transformed(dft_ref, *split))
    for a in range(antennas):
        o_ref[:, a, :, :] = spec[a].astype(jnp.bfloat16).reshape(
            o_ref.shape[0], o_ref.shape[2], o_ref.shape[3]
        )


def correlate_kernel(groups, blocks, antennas, channels, scale, y_ref, *refs):
    outs, scr, vis = refs[: blocks], refs[blocks], refs[blocks + 1]
    rows = antennas * channels * 2
    width = y_ref.shape[1]
    parts = width // LANES
    total = groups * blocks * antennas
    for g in range(groups):
        for q in range(blocks):
            src = y_ref[(g * blocks + q) * rows : (g * blocks + q + 1) * rows, :].astype(jnp.float32)
            for t in range(parts):
                scr[t, (q * groups + g) * rows : (q * groups + g + 1) * rows, :] = src[
                    :, t * LANES : (t + 1) * LANES
                ]
    for c in range(channels):
        re = [scr[t, pl.ds(2 * c, total, stride=2 * channels), :] for t in range(parts)]
        im = [scr[t, pl.ds(2 * c + 1, total, stride=2 * channels), :] for t in range(parts)]
        own = jnp.concatenate(re + im, axis=1).astype(jnp.bfloat16)
        turned = jnp.concatenate([-x for x in im] + re, axis=1).astype(jnp.bfloat16)
        both = jnp.concatenate([own, turned], axis=0)
        prod = times_transposed(own, both)
        vis[:, c, :, :] = (prod * scale).reshape(blocks, total // blocks, 2 * total)
    me = lax.axis_index("pair")
    for j in range(blocks):
        outs[j][...] = vis[me ^ j].astype(outs[j].dtype)


def place_kernel(blocks, *refs):
    ins, o_ref = refs[:blocks], refs[blocks]
    channels = ins[0].shape[0]
    columns = ins[0].shape[2] // 2
    me = lax.axis_index("pair")
    for j in range(blocks):
        at = pl.ds((me ^ j) * channels, channels)
        block = ins[j][...].astype(jnp.float32)
        o_ref[at, 0, :, :] = block[:, :, :columns]
        o_ref[at, 1, :, :] = block[:, :, columns:]


def exchanged_shards(groups, blocks, voltages, fir_taps):
    _, antennas, batches, length = voltages.shape
    taps, frame = fir_taps.shape
    frames = length // frame
    spectra = frames - taps + 1
    devices = groups * blocks
    channels = frame // 2 // devices
    total = devices * antennas
    table = dft_table(frame // 2)
    high = table.astype(jnp.bfloat16)
    table = jnp.asarray(np.stack([high, (table - high.astype(np.float64)).astype(jnp.bfloat16)]))
    vmem = pl.BlockSpec(memory_space=VMEM)
    hbm = pl.BlockSpec(memory_space=pltpu.MemorySpace.HBM)
    sent = pl.pallas_call(
        channelize_kernel,
        out_shape=jax.ShapeDtypeStruct(
            (devices, antennas, 2 * channels, batches * spectra), jnp.bfloat16
        ),
        in_specs=[hbm] * 3,
        out_specs=vmem,
        scratch_shapes=[
            pltpu.VMEM((antennas, batches, length), jnp.bfloat16),
            pltpu.VMEM((taps, frame), jnp.float32),
            pltpu.VMEM((2, frame, frame), jnp.bfloat16),
            pltpu.VMEM((antennas, batches, length // LANES, LANES), jnp.float32),
            pltpu.SemaphoreType.DMA((antennas + 2,)),
        ],
        compiler_params=pltpu.CompilerParams(vmem_limit_bytes=LIMIT),
        name="channelize",
    )(*[pltpu.with_memory_space_constraint(x, pltpu.MemorySpace.HBM) for x in (voltages[0], fir_taps, table)])
    sent = sent.reshape(devices, antennas * 2 * channels, batches * spectra)
    turned = lax.all_to_all(sent, ("chan", "pair"), 0, 0, tiled=True)
    piece = (channels, total // blocks, 2 * total)
    kinds = [jnp.float32 if j < 2 else jnp.bfloat16 for j in range(blocks)]
    pieces = pl.pallas_call(
        functools.partial(
            correlate_kernel,
            groups,
            blocks,
            antennas,
            channels,
            1.0 / math.sqrt(batches * spectra),
        ),
        out_shape=[jax.ShapeDtypeStruct(piece, kind) for kind in kinds],
        in_specs=[vmem],
        out_specs=[vmem] * blocks,
        scratch_shapes=[
            pltpu.VMEM(
                (batches * spectra // LANES, devices * antennas * 2 * channels, LANES), jnp.float32
            ),
            pltpu.VMEM((blocks, channels, total // blocks, 2 * total), jnp.float32),
        ],
        compiler_params=pltpu.CompilerParams(vmem_limit_bytes=LIMIT),
        name="correlate",
    )(turned.reshape(devices * antennas * 2 * channels, batches * spectra))
    arrived = [pieces[0]]
    for j in range(1, blocks):
        arrived.append(
            lax.ppermute(pieces[j], "pair", [(i, i ^ j) for i in range(blocks)])
        )
    return pl.pallas_call(
        functools.partial(place_kernel, blocks),
        out_shape=jax.ShapeDtypeStruct(
            (blocks * channels, 2, total // blocks, total), jnp.float32
        ),
        in_specs=[vmem] * blocks,
        out_specs=vmem,
        compiler_params=pltpu.CompilerParams(vmem_limit_bytes=LIMIT),
        name="place",
    )(*arrived)


def solution(mesh):
    groups, blocks = mesh.shape["chan"], mesh.shape["pair"]
    in_specs = (P("pair", "chan", None, None), P())
    out_specs = P("chan", None, "pair", None)

    def shards(voltages, fir_taps):
        channels = fir_taps.shape[1] // 2
        spectra = voltages.shape[3] // fir_taps.shape[1] - fir_taps.shape[0] + 1
        if (
            channels % (groups * blocks) == 0
            and blocks & (blocks - 1) == 0
            and fir_taps.shape[1] % LANES == 0
            and spectra % LANES == 0
            and voltages.shape[1] * 2 * channels // (groups * blocks) % 16 == 0
        ):
            return exchanged_shards(groups, blocks, voltages, fir_taps)
        return gathered_shards(voltages, fir_taps)

    return jax.shard_map(shards, mesh=mesh, in_specs=in_specs, out_specs=out_specs, check_vma=False)
```

```python
import functools
import math

import jax
import jax.numpy as jnp
import numpy as np
from jax import lax
from jax.experimental import pallas as pl
from jax.experimental.pallas import tpu as pltpu
from jax.sharding import PartitionSpec as P


LANES = 128
LIMIT = 16 * 2**20
VMEM = pltpu.MemorySpace.VMEM


def dft_rows(channels):
    frame = 2 * channels
    row_index = jnp.arange(2 * channels, dtype=jnp.int32)
    col_index = jnp.arange(frame, dtype=jnp.int32)
    freq_index = row_index // 2
    phases = freq_index[:, None] * col_index[None, :] % frame
    angles = phases.astype(jnp.float32) * (2.0 * math.pi / frame)
    chosen = jnp.where((row_index % 2 == 0)[:, None], jnp.cos(angles), -jnp.sin(angles))
    return chosen * (1.0 / math.sqrt(frame))


def dft_table(channels):
    frame = 2 * channels
    row = np.arange(frame)
    phases = (row // 2)[:, None] * np.arange(frame)[None, :] % frame
    angles = phases * (2.0 * np.pi / frame)
    chosen = np.where((row % 2 == 0)[:, None], np.cos(angles), -np.sin(angles))
    return chosen / np.sqrt(frame)


def channelize(sample_rows, fir_taps, transform, spectra_len):
    tap_count, frame = fir_taps.shape
    channels = frame // 2
    framed = sample_rows.astype(jnp.float32).reshape(
        sample_rows.shape[0], spectra_len + tap_count - 1, frame
    )
    filtered = jnp.zeros((sample_rows.shape[0], spectra_len, frame), jnp.float32)
    for tap in range(tap_count):
        filtered = filtered + fir_taps[tap][None, None, :] * framed[:, tap : tap + spectra_len, :]
    spectra = jnp.einsum("wn,asn->aws", transform, filtered, precision=lax.Precision.HIGHEST)
    return spectra.reshape(sample_rows.shape[0], channels, 2 * spectra_len).astype(jnp.bfloat16)


def correlate(own_rows, columns, spectra_len):
    blocks = columns.shape[2] // (2 * spectra_len)
    shaped = columns.reshape(columns.shape[0], columns.shape[1], blocks, 2, spectra_len)
    rotated = jnp.stack([-shaped[:, :, :, 1, :], shaped[:, :, :, 0, :]], axis=3).reshape(
        columns.shape
    )
    stacked = jnp.concatenate([columns, rotated], axis=0)
    stacked = jnp.transpose(stacked, (1, 0, 2))
    own_first = jnp.transpose(own_rows, (1, 0, 2))
    product = jnp.einsum("cik,cjk->cij", own_first, stacked, preferred_element_type=jnp.float32)
    count = columns.shape[0]
    product = product.reshape(product.shape[0], product.shape[1], 2, count)
    return jnp.transpose(product, (0, 2, 1, 3))


def gathered_shards(voltages, fir_taps):
    samples = voltages[0]
    batch_count = samples.shape[1]
    tap_count, frame = fir_taps.shape
    spectra_len = samples.shape[2] // frame - tap_count + 1
    transform = dft_rows(frame // 2)
    pieces = [
        channelize(samples[:, batch], fir_taps, transform, spectra_len)
        for batch in range(batch_count)
    ]
    spectra = jnp.concatenate(pieces, axis=2)[None]
    turned = lax.all_to_all(spectra, "chan", split_axis=2, concat_axis=1, tiled=True)
    own_rows = turned[0]
    arrived = lax.all_gather(turned, "pair", axis=0, tiled=True)
    flat = arrived.reshape(arrived.shape[0] * arrived.shape[1], arrived.shape[2], arrived.shape[3])
    summed = correlate(own_rows, flat, spectra_len)
    return summed * (1.0 / math.sqrt(batch_count * spectra_len))


def times_transposed(left, right):
    return lax.dot_general(
        left, right, (((1,), (1,)), ((), ())), preferred_element_type=jnp.float32
    )


def transformed(dft_ref, high, low):
    total = times_transposed(dft_ref[0], high) + times_transposed(dft_ref[1], high)
    return total + times_transposed(dft_ref[0], low)


def channelize_kernel(v_hbm, taps_hbm, dft_hbm, o_ref, v_ref, taps_ref, dft_ref, x_ref, sems):
    antennas, batches, length = v_ref.shape
    taps, frame = taps_ref.shape
    copies = [pltpu.make_async_copy(v_hbm.at[a], v_ref.at[a], sems.at[a]) for a in range(antennas)]
    copy_taps = pltpu.make_async_copy(taps_hbm, taps_ref, sems.at[antennas])
    copy_dft = pltpu.make_async_copy(dft_hbm, dft_ref, sems.at[antennas + 1])
    for copy in copies + [copy_taps, copy_dft]:
        copy.start()
    copy_taps.wait()
    parts = frame // LANES
    spectra = length // frame - taps + 1
    spec = []
    for a in range(antennas):
        copies[a].wait()
        if a == 1 or antennas == 1:
            copy_dft.wait()
        if a > 0:
            spec.append(transformed(dft_ref, *split))
        samples = v_ref[a].astype(jnp.float32)
        for b in range(batches):
            x_ref[a, b] = samples[b].reshape(length // LANES, LANES)
        filtered = []
        for b in range(batches):
            row = []
            for h in range(parts):
                lanes = slice(h * LANES, (h + 1) * LANES)
                total = None
                for p in range(taps):
                    rows = x_ref[a, b, pl.ds(p * parts + h, spectra, stride=parts), :]
                    term = taps_ref[p : p + 1, lanes] * rows
                    total = term if total is None else total + term
                high = total.astype(jnp.bfloat16)
                row.append((high, (total - high.astype(jnp.float32)).astype(jnp.bfloat16)))
            filtered.append(row)
        split = [
            jnp.concatenate([jnp.concatenate([x[n] for x in row], axis=1) for row in filtered], axis=0)
            for n in range(2)
        ]
    spec.append(transformed(dft_ref, *split))
    for a in range(antennas):
        o_ref[:, a, :, :] = spec[a].astype(jnp.bfloat16).reshape(
            o_ref.shape[0], o_ref.shape[2], o_ref.shape[3]
        )


def correlate_kernel(groups, blocks, antennas, channels, scale, y_ref, *refs):
    outs, scr, vis = refs[: blocks], refs[blocks], refs[blocks + 1]
    rows = antennas * channels * 2
    width = y_ref.shape[1]
    parts = width // LANES
    total = groups * blocks * antennas
    for g in range(groups):
        for q in range(blocks):
            src = y_ref[(g * blocks + q) * rows : (g * blocks + q + 1) * rows, :].astype(jnp.float32)
            for t in range(parts):
                scr[t, (q * groups + g) * rows : (q * groups + g + 1) * rows, :] = src[
                    :, t * LANES : (t + 1) * LANES
                ]
    gathered = []
    for c in range(channels):
        re = [scr[t, pl.ds(2 * c, total, stride=2 * channels), :] for t in range(parts)]
        im = [scr[t, pl.ds(2 * c + 1, total, stride=2 * channels), :] for t in range(parts)]
        own = jnp.concatenate(re + im, axis=1).astype(jnp.bfloat16)
        turned = jnp.concatenate([-x for x in im] + re, axis=1).astype(jnp.bfloat16)
        gathered.append((own, jnp.concatenate([own, turned], axis=0)))
    for c, (own, both) in enumerate(gathered):
        prod = times_transposed(own[:, :width], both[:, :width])
        prod = prod + times_transposed(own[:, width:], both[:, width:])
        vis[:, c, :, :] = (prod * scale).reshape(blocks, total // blocks, 2 * total)
    me = lax.axis_index("pair")
    for j in range(blocks):
        outs[j][...] = vis[me ^ j].astype(outs[j].dtype)


def place_kernel(blocks, *refs):
    ins, o_ref = refs[:blocks], refs[blocks]
    channels = ins[0].shape[0]
    columns = ins[0].shape[2] // 2
    me = lax.axis_index("pair")
    for j in range(blocks):
        at = pl.ds((me ^ j) * channels, channels)
        block = ins[j][...].astype(jnp.float32)
        o_ref[at, 0, :, :] = block[:, :, :columns]
        o_ref[at, 1, :, :] = block[:, :, columns:]


def exchanged_shards(groups, blocks, voltages, fir_taps):
    _, antennas, batches, length = voltages.shape
    taps, frame = fir_taps.shape
    frames = length // frame
    spectra = frames - taps + 1
    devices = groups * blocks
    channels = frame // 2 // devices
    total = devices * antennas
    table = dft_table(frame // 2)
    high = table.astype(jnp.bfloat16)
    table = jnp.asarray(np.stack([high, (table - high.astype(np.float64)).astype(jnp.bfloat16)]))
    vmem = pl.BlockSpec(memory_space=VMEM)
    hbm = pl.BlockSpec(memory_space=pltpu.MemorySpace.HBM)
    sent = pl.pallas_call(
        channelize_kernel,
        out_shape=jax.ShapeDtypeStruct(
            (devices, antennas, 2 * channels, batches * spectra), jnp.bfloat16
        ),
        in_specs=[hbm] * 3,
        out_specs=vmem,
        scratch_shapes=[
            pltpu.VMEM((antennas, batches, length), jnp.bfloat16),
            pltpu.VMEM((taps, frame), jnp.float32),
            pltpu.VMEM((2, frame, frame), jnp.bfloat16),
            pltpu.VMEM((antennas, batches, length // LANES, LANES), jnp.float32),
            pltpu.SemaphoreType.DMA((antennas + 2,)),
        ],
        compiler_params=pltpu.CompilerParams(vmem_limit_bytes=LIMIT),
        name="channelize",
    )(*[pltpu.with_memory_space_constraint(x, pltpu.MemorySpace.HBM) for x in (voltages[0], fir_taps, table)])
    sent = sent.reshape(devices, antennas * 2 * channels, batches * spectra)
    turned = lax.all_to_all(sent, ("chan", "pair"), 0, 0, tiled=True)
    piece = (channels, total // blocks, 2 * total)
    kinds = [jnp.float32 if j < 2 else jnp.bfloat16 for j in range(blocks)]
    pieces = pl.pallas_call(
        functools.partial(
            correlate_kernel,
            groups,
            blocks,
            antennas,
            channels,
            1.0 / math.sqrt(batches * spectra),
        ),
        out_shape=[jax.ShapeDtypeStruct(piece, kind) for kind in kinds],
        in_specs=[vmem],
        out_specs=[vmem] * blocks,
        scratch_shapes=[
            pltpu.VMEM(
                (batches * spectra // LANES, devices * antennas * 2 * channels, LANES), jnp.float32
            ),
            pltpu.VMEM((blocks, channels, total // blocks, 2 * total), jnp.float32),
        ],
        compiler_params=pltpu.CompilerParams(vmem_limit_bytes=LIMIT),
        name="correlate",
    )(turned.reshape(devices * antennas * 2 * channels, batches * spectra))
    arrived = [pieces[0]]
    for j in range(1, blocks):
        arrived.append(
            lax.ppermute(pieces[j], "pair", [(i, i ^ j) for i in range(blocks)])
        )
    return pl.pallas_call(
        functools.partial(place_kernel, blocks),
        out_shape=jax.ShapeDtypeStruct(
            (blocks * channels, 2, total // blocks, total), jnp.float32
        ),
        in_specs=[vmem] * blocks,
        out_specs=vmem,
        compiler_params=pltpu.CompilerParams(vmem_limit_bytes=LIMIT),
        name="place",
    )(*arrived)


def solution(mesh):
    groups, blocks = mesh.shape["chan"], mesh.shape["pair"]
    in_specs = (P("pair", "chan", None, None), P())
    out_specs = P("chan", None, "pair", None)

    def shards(voltages, fir_taps):
        channels = fir_taps.shape[1] // 2
        spectra = voltages.shape[3] // fir_taps.shape[1] - fir_taps.shape[0] + 1
        if (
            channels % (groups * blocks) == 0
            and blocks & (blocks - 1) == 0
            and fir_taps.shape[1] % LANES == 0
            and spectra % LANES == 0
            and voltages.shape[1] * 2 * channels // (groups * blocks) % 16 == 0
        ):
            return exchanged_shards(groups, blocks, voltages, fir_taps)
        return gathered_shards(voltages, fir_taps)

    return jax.shard_map(shards, mesh=mesh, in_specs=in_specs, out_specs=out_specs, check_vma=False)
```

```python
import functools
import math

import jax
import jax.numpy as jnp
import numpy as np
from jax import lax
from jax.experimental import pallas as pl
from jax.experimental.pallas import tpu as pltpu
from jax.sharding import PartitionSpec as P


LANES = 128
LIMIT = 16 * 2**20
VMEM = pltpu.MemorySpace.VMEM


def dft_rows(channels):
    frame = 2 * channels
    row_index = jnp.arange(2 * channels, dtype=jnp.int32)
    col_index = jnp.arange(frame, dtype=jnp.int32)
    freq_index = row_index // 2
    phases = freq_index[:, None] * col_index[None, :] % frame
    angles = phases.astype(jnp.float32) * (2.0 * math.pi / frame)
    chosen = jnp.where((row_index % 2 == 0)[:, None], jnp.cos(angles), -jnp.sin(angles))
    return chosen * (1.0 / math.sqrt(frame))


def dft_table(channels):
    frame = 2 * channels
    row = np.arange(frame)
    phases = (row // 2)[:, None] * np.arange(frame)[None, :] % frame
    angles = phases * (2.0 * np.pi / frame)
    chosen = np.where((row % 2 == 0)[:, None], np.cos(angles), -np.sin(angles))
    return chosen / np.sqrt(frame)


def channelize(sample_rows, fir_taps, transform, spectra_len):
    tap_count, frame = fir_taps.shape
    channels = frame // 2
    framed = sample_rows.astype(jnp.float32).reshape(
        sample_rows.shape[0], spectra_len + tap_count - 1, frame
    )
    filtered = jnp.zeros((sample_rows.shape[0], spectra_len, frame), jnp.float32)
    for tap in range(tap_count):
        filtered = filtered + fir_taps[tap][None, None, :] * framed[:, tap : tap + spectra_len, :]
    spectra = jnp.einsum("wn,asn->aws", transform, filtered, precision=lax.Precision.HIGHEST)
    return spectra.reshape(sample_rows.shape[0], channels, 2 * spectra_len).astype(jnp.bfloat16)


def correlate(own_rows, columns, spectra_len):
    blocks = columns.shape[2] // (2 * spectra_len)
    shaped = columns.reshape(columns.shape[0], columns.shape[1], blocks, 2, spectra_len)
    rotated = jnp.stack([-shaped[:, :, :, 1, :], shaped[:, :, :, 0, :]], axis=3).reshape(
        columns.shape
    )
    stacked = jnp.concatenate([columns, rotated], axis=0)
    stacked = jnp.transpose(stacked, (1, 0, 2))
    own_first = jnp.transpose(own_rows, (1, 0, 2))
    product = jnp.einsum("cik,cjk->cij", own_first, stacked, preferred_element_type=jnp.float32)
    count = columns.shape[0]
    product = product.reshape(product.shape[0], product.shape[1], 2, count)
    return jnp.transpose(product, (0, 2, 1, 3))


def gathered_shards(voltages, fir_taps):
    samples = voltages[0]
    batch_count = samples.shape[1]
    tap_count, frame = fir_taps.shape
    spectra_len = samples.shape[2] // frame - tap_count + 1
    transform = dft_rows(frame // 2)
    pieces = [
        channelize(samples[:, batch], fir_taps, transform, spectra_len)
        for batch in range(batch_count)
    ]
    spectra = jnp.concatenate(pieces, axis=2)[None]
    turned = lax.all_to_all(spectra, "chan", split_axis=2, concat_axis=1, tiled=True)
    own_rows = turned[0]
    arrived = lax.all_gather(turned, "pair", axis=0, tiled=True)
    flat = arrived.reshape(arrived.shape[0] * arrived.shape[1], arrived.shape[2], arrived.shape[3])
    summed = correlate(own_rows, flat, spectra_len)
    return summed * (1.0 / math.sqrt(batch_count * spectra_len))


def times_transposed(left, right):
    return lax.dot_general(
        left, right, (((1,), (1,)), ((), ())), preferred_element_type=jnp.float32
    )


def transformed(dft_ref, high, low):
    total = times_transposed(dft_ref[0], high) + times_transposed(dft_ref[1], high)
    return total + times_transposed(dft_ref[0], low)


def channelize_kernel(v_hbm, taps_hbm, dft_hbm, o_ref, v_ref, taps_ref, dft_ref, x_ref, sems):
    antennas, batches, length = v_ref.shape
    taps, frame = taps_ref.shape
    copies = [pltpu.make_async_copy(v_hbm.at[a], v_ref.at[a], sems.at[a]) for a in range(antennas)]
    copy_taps = pltpu.make_async_copy(taps_hbm, taps_ref, sems.at[antennas])
    copy_dft = pltpu.make_async_copy(dft_hbm, dft_ref, sems.at[antennas + 1])
    for copy in copies + [copy_taps, copy_dft]:
        copy.start()
    copy_taps.wait()
    parts = frame // LANES
    spectra = length // frame - taps + 1
    spec = []
    for a in range(antennas):
        copies[a].wait()
        if a == 1 or antennas == 1:
            copy_dft.wait()
        if a > 0:
            spec.append(transformed(dft_ref, *split))
        samples = v_ref[a].astype(jnp.float32)
        for b in range(batches):
            x_ref[a, b] = samples[b].reshape(length // LANES, LANES)
        filtered = []
        for b in range(batches):
            row = []
            for h in range(parts):
                lanes = slice(h * LANES, (h + 1) * LANES)
                total = None
                for p in range(taps):
                    rows = x_ref[a, b, pl.ds(p * parts + h, spectra, stride=parts), :]
                    term = taps_ref[p : p + 1, lanes] * rows
                    total = term if total is None else total + term
                high = total.astype(jnp.bfloat16)
                row.append((high, (total - high.astype(jnp.float32)).astype(jnp.bfloat16)))
            filtered.append(row)
        split = [
            jnp.concatenate([jnp.concatenate([x[n] for x in row], axis=1) for row in filtered], axis=0)
            for n in range(2)
        ]
    spec.append(transformed(dft_ref, *split))
    for a in range(antennas):
        o_ref[:, a, :, :] = spec[a].astype(jnp.bfloat16).reshape(
            o_ref.shape[0], o_ref.shape[2], o_ref.shape[3]
        )


def correlate_kernel(groups, blocks, antennas, channels, scale, y_ref, *refs):
    outs, scr, vis = refs[: blocks], refs[blocks], refs[blocks + 1]
    rows = antennas * channels * 2
    width = y_ref.shape[1]
    parts = width // LANES
    total = groups * blocks * antennas
    for g in range(groups):
        for q in range(blocks):
            src = y_ref[(g * blocks + q) * rows : (g * blocks + q + 1) * rows, :].astype(jnp.float32)
            for t in range(parts):
                scr[t, (q * groups + g) * rows : (q * groups + g + 1) * rows, :] = src[
                    :, t * LANES : (t + 1) * LANES
                ]
    for c in range(channels):
        re = [scr[t, pl.ds(2 * c, total, stride=2 * channels), :] for t in range(parts)]
        im = [scr[t, pl.ds(2 * c + 1, total, stride=2 * channels), :] for t in range(parts)]
        own = jnp.concatenate(re + im, axis=1).astype(jnp.bfloat16)
        turned = jnp.concatenate([-x for x in im] + re, axis=1).astype(jnp.bfloat16)
        both = jnp.concatenate([own, turned], axis=0)
        prod = times_transposed(own, both)
        vis[:, c, :, :] = (prod * scale).reshape(blocks, total // blocks, 2 * total)
    me = lax.axis_index("pair")
    for j in range(blocks):
        outs[j][...] = vis[me ^ j].astype(outs[j].dtype)


def place_kernel(steps, *refs):
    ins, (o_hbm, buf, sems) = refs[: len(steps)], refs[-3:]
    channels = ins[0].shape[0]
    columns = ins[0].shape[2] // 2
    me = lax.axis_index("pair")
    copies = []
    for n, j in enumerate(steps):
        block = ins[n][...].astype(jnp.float32)
        buf[n, :, 0] = block[:, :, :columns]
        buf[n, :, 1] = block[:, :, columns:]
        at = pl.ds((me ^ j) * channels, channels)
        copies.append(pltpu.make_async_copy(buf.at[n], o_hbm.at[at], sems.at[n]))
        copies[-1].start()
    for copy in copies:
        copy.wait()


def exchanged_shards(groups, blocks, voltages, fir_taps):
    _, antennas, batches, length = voltages.shape
    taps, frame = fir_taps.shape
    frames = length // frame
    spectra = frames - taps + 1
    devices = groups * blocks
    channels = frame // 2 // devices
    total = devices * antennas
    table = dft_table(frame // 2)
    high = table.astype(jnp.bfloat16)
    table = jnp.asarray(np.stack([high, (table - high.astype(np.float64)).astype(jnp.bfloat16)]))
    vmem = pl.BlockSpec(memory_space=VMEM)
    hbm = pl.BlockSpec(memory_space=pltpu.MemorySpace.HBM)
    sent = pl.pallas_call(
        channelize_kernel,
        out_shape=jax.ShapeDtypeStruct(
            (devices, antennas, 2 * channels, batches * spectra), jnp.bfloat16
        ),
        in_specs=[hbm] * 3,
        out_specs=vmem,
        scratch_shapes=[
            pltpu.VMEM((antennas, batches, length), jnp.bfloat16),
            pltpu.VMEM((taps, frame), jnp.float32),
            pltpu.VMEM((2, frame, frame), jnp.bfloat16),
            pltpu.VMEM((antennas, batches, length // LANES, LANES), jnp.float32),
            pltpu.SemaphoreType.DMA((antennas + 2,)),
        ],
        compiler_params=pltpu.CompilerParams(vmem_limit_bytes=LIMIT),
        name="channelize",
    )(*[pltpu.with_memory_space_constraint(x, pltpu.MemorySpace.HBM) for x in (voltages[0], fir_taps, table)])
    sent = sent.reshape(devices, antennas * 2 * channels, batches * spectra)
    turned = lax.all_to_all(sent, ("chan", "pair"), 0, 0, tiled=True)
    piece = (channels, total // blocks, 2 * total)
    kinds = [jnp.float32 if j < 2 else jnp.bfloat16 for j in range(blocks)]
    pieces = pl.pallas_call(
        functools.partial(
            correlate_kernel,
            groups,
            blocks,
            antennas,
            channels,
            1.0 / math.sqrt(batches * spectra),
        ),
        out_shape=[jax.ShapeDtypeStruct(piece, kind) for kind in kinds],
        in_specs=[vmem],
        out_specs=[vmem] * blocks,
        scratch_shapes=[
            pltpu.VMEM(
                (batches * spectra // LANES, devices * antennas * 2 * channels, LANES), jnp.float32
            ),
            pltpu.VMEM((blocks, channels, total // blocks, 2 * total), jnp.float32),
        ],
        compiler_params=pltpu.CompilerParams(vmem_limit_bytes=LIMIT),
        name="correlate",
    )(turned.reshape(devices * antennas * 2 * channels, batches * spectra))
    arrived = [pieces[0]]
    for j in range(1, blocks):
        arrived.append(
            lax.ppermute(pieces[j], "pair", [(i, i ^ j) for i in range(blocks)])
        )
    shape = (channels, 2, total // blocks, total)

    def placed(steps, into):
        return pl.pallas_call(
            functools.partial(place_kernel, steps),
            out_shape=jax.ShapeDtypeStruct((blocks * channels,) + shape[1:], jnp.float32),
            in_specs=[vmem] * len(steps) + [hbm] * len(into),
            out_specs=hbm,
            scratch_shapes=[
                pltpu.VMEM((len(steps),) + shape, jnp.float32),
                pltpu.SemaphoreType.DMA((len(steps),)),
            ],
            input_output_aliases={len(steps): 0} if into else {},
            compiler_params=pltpu.CompilerParams(vmem_limit_bytes=LIMIT),
        )(*[arrived[j] for j in steps], *into)

    near, far = [0], list(range(1, blocks))
    out = placed(near, [])
    return placed(far, [out]) if far else out


def solution(mesh):
    groups, blocks = mesh.shape["chan"], mesh.shape["pair"]
    in_specs = (P("pair", "chan", None, None), P())
    out_specs = P("chan", None, "pair", None)

    def shards(voltages, fir_taps):
        channels = fir_taps.shape[1] // 2
        spectra = voltages.shape[3] // fir_taps.shape[1] - fir_taps.shape[0] + 1
        if (
            channels % (groups * blocks) == 0
            and blocks & (blocks - 1) == 0
            and fir_taps.shape[1] % LANES == 0
            and spectra % LANES == 0
            and voltages.shape[1] * 2 * channels // (groups * blocks) % 16 == 0
        ):
            return exchanged_shards(groups, blocks, voltages, fir_taps)
        return gathered_shards(voltages, fir_taps)

    return jax.shard_map(shards, mesh=mesh, in_specs=in_specs, out_specs=out_specs, check_vma=False)
```
